32 devices in a mesh: fsdp: 4 (over x, core), ctx: 2 (over y), tp: 4 (over z).
Axes of the slice: x: 2, y: 2, z: 4, core: 2. Of those that a mesh axis runs over, the one named last changes fastest.
Arguments:
- layer_in: bfloat16 [16, 512, 1024], P('fsdp', ('ctx', 'tp')), may hold values from -6 to 6
- lengths: int32 [16], P('fsdp'), may hold values from 128 to 512, as said below
- cotangent: bfloat16 [16, 512, 1024], P('fsdp', ('ctx', 'tp')), may hold values from -6 to 6
- w_query: bfloat16 [1024, 1024], P('fsdp', 'tp'), may hold values from -0.1875 to 0.1875
- w_key: bfloat16 [1024, 1024], P('fsdp', 'tp'), may hold values from -0.1875 to 0.1875
- w_value: bfloat16 [1024, 1024], P('fsdp', 'tp'), may hold values from -0.1875 to 0.1875
- b_query: bfloat16 [1024], P(('tp', 'fsdp')), may hold values from -0.59765625 to 0.59765625
- b_value: bfloat16 [1024], P(('tp', 'fsdp')), may hold values from -0.29882812 to 0.29882812
- w_out: bfloat16 [1024, 1024], P('tp', 'fsdp'), may hold values from -2 to 2
- b_out: bfloat16 [1024], P('fsdp'), may hold values from -0.59765625 to 0.59765625
- gain_attn: bfloat16 [1024], P('fsdp'), may hold values from 0.099609375 to 1.8984375
- shift_attn: bfloat16 [1024], P('fsdp'), may hold values from -0.59765625 to 0.59765625
- w_up: bfloat16 [1024, 4096], P('fsdp', 'tp'), may hold values from -0.1875 to 0.1875
- b_up: bfloat16 [4096], P(('tp', 'fsdp')), may hold values from -0.59765625 to 0.59765625
- w_down: bfloat16 [4096, 1024], P('tp', 'fsdp'), may hold values from -0.09375 to 0.09375
- b_down: bfloat16 [1024], P('fsdp'), may hold values from -0.59765625 to 0.59765625
- gain_ffn: bfloat16 [1024], P('fsdp'), may hold values from 0.099609375 to 1.8984375
- shift_ffn: bfloat16 [1024], P('fsdp'), may hold values from -0.59765625 to 0.59765625
Outputs:
- layer_out: bfloat16 [16, 512, 1024], P('fsdp', ('ctx', 'tp'))
- input_grad: bfloat16 [16, 512, 1024], P('fsdp', ('ctx', 'tp'))
- grad_w_query: float32 [1024, 1024], P('fsdp', 'tp')
- grad_w_key: float32 [1024, 1024], P('fsdp', 'tp')
- grad_w_value: float32 [1024, 1024], P('fsdp', 'tp')
- grad_b_query: float32 [1024], P(('tp', 'fsdp'))
- grad_b_value: float32 [1024], P(('tp', 'fsdp'))
- grad_w_out: float32 [1024, 1024], P('tp', 'fsdp')
- grad_b_out: float32 [1024], P('fsdp')
- grad_gain_attn: float32 [1024], P('fsdp')
- grad_shift_attn: float32 [1024], P('fsdp')
- grad_w_up: float32 [1024, 4096], P('fsdp', 'tp')
- grad_b_up: float32 [4096], P(('tp', 'fsdp'))
- grad_w_down: float32 [4096, 1024], P('tp', 'fsdp')
- grad_b_down: float32 [1024], P('fsdp')
- grad_gain_ffn: float32 [1024], P('fsdp')
- grad_shift_ffn: float32 [1024], P('fsdp')
The draws below stay inside these ranges and needn't reach their ends.
Inputs may be any that keep to these rules, and one draw needn't show every extreme that they name: Slots 0 to lengths - 1 of a sequence are valid. One sequence has exactly 512 valid slots and one exactly 128.
All inputs are finite; a program needn't handle non-finite values.
Results may differ from the reference program's by a relative error of at most 0.024.
Values may be sent and summed in bfloat16 or wider, within the bound.
No kernel may reach another device: no remote copies, remote signals or barrier semaphores. Data moves between devices by JAX's collectives and lax.ppermute only.
A program may use at most 128 MiB of HBM per device.

```python
import math
import jax
import jax.numpy as jnp
from jax import lax

D = 1024
FF = 4096
HEADS = 16
DH = 64
SLOTS = 512
MIN_LEN = 128
SEQS = 16


def draw_lengths(key, part):
    drawn = jax.random.randint(jax.random.fold_in(key, 11), (SEQS,), MIN_LEN, SLOTS + 1)
    order = jax.random.permutation(jax.random.fold_in(key, 12), SEQS)
    drawn = drawn.at[order[0]].set(SLOTS)
    drawn = drawn.at[order[1]].set(MIN_LEN)
    return drawn.astype(jnp.int32)


def spiked(array, own_key, source, target, blocks, factor):
    owner, partner = [(jnp.arange(array.shape[axis_at]) // (array.shape[axis_at] // blocks)).reshape([-1 if axis == axis_at else 1 for axis in range(array.ndim)]) for axis_at in (source, target)]
    chosen = jax.random.permutation(own_key, blocks)[partner]
    strong = (owner == chosen) | (owner == (partner + blocks // 2) % blocks)
    return jnp.where(strong, factor * array, array)


def shard_levels(stream_key, shape, cuts, least, top_value):
    gain, own = 1.0, jax.random.fold_in(stream_key, 6)
    for axis_at, parts in cuts:
        draws = jnp.exp(jax.random.uniform(jax.random.fold_in(own, axis_at), (parts,), jnp.float32, least / len(cuts), top_value / len(cuts)))
        gain = gain * jnp.repeat(draws, shape[axis_at] // parts).reshape([-1 if axis == axis_at else 1 for axis in range(len(shape))])
    return gain


def normal_values(rng, dims, scale, bound, pieces=(), dtype=jnp.bfloat16):
    values = scale * jax.random.normal(rng, dims, jnp.float32)
    if pieces:
        values = values * shard_levels(rng, dims, pieces, -0.22, 0.18)
    return jnp.clip(values, -bound, bound).astype(dtype)


def bell_draw_with(own_key, shape, spread, most, cuts, heavy, held_as=jnp.bfloat16):
    entries = spread * jax.random.normal(own_key, shape, jnp.float32)
    if cuts:
        entries = entries * shard_levels(own_key, shape, cuts, -0.22, 0.18)
    return jnp.clip(spiked(entries, jax.random.fold_in(own_key, 3), *heavy), -most, most).astype(held_as)


def setup_inputs(seed: int = 0) -> dict:
    arg_keys = jax.random.split(jax.random.key(seed), 19)
    return {
        "layer_in": normal_values(arg_keys[0], (SEQS, SLOTS, D), 1.0, 6.0, ((0, 4), (1, 8))),
        "lengths": draw_lengths(jax.random.fold_in(arg_keys[18], 71), 0),
        "cotangent": bell_draw_with(arg_keys[2], (SEQS, SLOTS, D), 1.0, 6.0, ((0, 4), (1, 8)), (0, 2, 4, 2.0)),
        "w_query": normal_values(arg_keys[3], (D, D), D ** -0.5, 0.1875, ((0, 4), (1, 4))),
        "w_key": normal_values(arg_keys[4], (D, D), D ** -0.5, 0.1875, ((0, 4), (1, 4))),
        "w_value": normal_values(arg_keys[5], (D, D), D ** -0.5, 0.1875, ((0, 4), (1, 4))),
        "b_query": normal_values(arg_keys[6], (D,), 0.1, 0.59765625, ((0, 16),)),
        "b_value": normal_values(arg_keys[7], (D,), 0.05, 0.29882812, ((0, 16),)),
        "w_out": normal_values(arg_keys[8], (D, D), (D // 128) ** -0.5, 2.0, ((0, 4), (1, 4))),
        "b_out": normal_values(arg_keys[9], (D,), 0.1, 0.59765625, ((0, 4),)),
        "gain_attn": jnp.clip(1.0 + 0.18 * jax.random.normal(arg_keys[10], (D,), jnp.float32), 0.099609375, 1.8984375).astype(jnp.bfloat16),
        "shift_attn": normal_values(arg_keys[11], (D,), 0.1, 0.59765625, ((0, 4),)),
        "w_up": normal_values(arg_keys[12], (D, FF), D ** -0.5, 0.1875, ((0, 4), (1, 4))),
        "b_up": normal_values(arg_keys[13], (FF,), 0.1, 0.59765625, ((0, 16),)),
        "w_down": normal_values(arg_keys[14], (FF, D), FF ** -0.5, 0.09375, ((0, 4), (1, 4))),
        "b_down": normal_values(arg_keys[15], (D,), 0.1, 0.59765625, ((0, 4),)),
        "gain_ffn": jnp.clip(1.0 + 0.18 * jax.random.normal(arg_keys[16], (D,), jnp.float32), 0.099609375, 1.8984375).astype(jnp.bfloat16),
        "shift_ffn": normal_values(arg_keys[17], (D,), 0.1, 0.59765625, ((0, 4),)),
    }


PRECISE = lax.Precision.HIGHEST
EPSILON = 1e-12
MASKED = -1000000000.0

@jax.custom_vjp
def low(v):
    return lax.optimization_barrier(v.astype(jnp.bfloat16)).astype(jnp.float32)

@jax.custom_vjp
def low_back(v):
    return v

def low_keep(v):
    return (low(v), None)

def low_pass(kept, grad):
    return (grad,)

def back_keep(v):
    return (v, None)

def back_low(kept, grad):
    return (low(grad),)
low.defvjp(low_keep, low_pass)
low_back.defvjp(back_keep, back_low)

def matmul(left, right):
    return jnp.dot(left, right, precision=PRECISE, preferred_element_type=jnp.float32)

def normalize(row_data, gain_vec, shift_vec):
    row_mean = lax.optimization_barrier(jnp.mean(row_data, axis=-1, keepdims=True))
    centered = row_data - row_mean
    row_var = lax.optimization_barrier(jnp.mean(centered * centered, axis=-1, keepdims=True))
    return centered * lax.rsqrt(row_var + EPSILON) * gain_vec + shift_vec

def block_forward(weights, block_rows, seq_lengths):
    w_query, w_key, w_value, b_query, b_value, w_out, b_out, gain_attn, shift_attn, w_up, b_up, w_down, b_down, gain_ffn, shift_ffn = weights
    group_size, slot_count, model_width = block_rows.shape
    flat_rows = block_rows.reshape(group_size * slot_count, model_width)
    queries = low_back(low(matmul(flat_rows, w_query) + b_query)).reshape(group_size, slot_count, HEADS, DH)
    key_heads = low_back(low(matmul(flat_rows, w_key))).reshape(group_size, slot_count, HEADS, DH)
    value_heads = low_back(low(matmul(flat_rows, w_value) + b_value)).reshape(group_size, slot_count, HEADS, DH)
    raw_scores = jnp.einsum('gqhd,gkhd->ghqk', queries, key_heads, precision=PRECISE) * DH ** (-0.5)
    scores = low_back(raw_scores)
    key_valid = lax.broadcasted_iota(jnp.int32, (group_size, slot_count), 1) < seq_lengths[:, None]
    scores = jnp.where(key_valid[:, None, None, :], scores, MASKED)
    row_top = lax.optimization_barrier(jnp.max(scores, axis=-1, keepdims=True))
    exp_scores = jnp.exp(scores - row_top)
    attn_probs = exp_scores / lax.optimization_barrier(jnp.sum(exp_scores, axis=-1, keepdims=True))
    probs_low = low_back(low(attn_probs))
    mixed = jnp.einsum('ghqk,gkhd->gqhd', probs_low, value_heads, precision=PRECISE)
    attn_rows = low_back(low(mixed.reshape(group_size * slot_count, model_width)))
    projected = low_back(matmul(attn_rows, w_out) + b_out)
    resid_one = flat_rows + projected
    normed_one = normalize(resid_one, gain_attn, shift_attn)
    normed_low = low(normed_one)
    hidden_pre = low_back(matmul(normed_low, w_up) + b_up)
    hidden = low(jax.nn.gelu(hidden_pre, approximate=False))
    ffn_out = low_back(matmul(hidden, w_down) + b_down)
    resid_two = normed_one + ffn_out
    return normalize(resid_two, gain_ffn, shift_ffn).reshape(group_size, slot_count, model_width)

def reference(layer_in, lengths, cotangent, w_query, w_key, w_value, b_query, b_value, w_out, b_out, gain_attn, shift_attn, w_up, b_up, w_down, b_down, gain_ffn, shift_ffn):
    weights = tuple((array_in.astype(jnp.float32) for array_in in (w_query, w_key, w_value, b_query, b_value, w_out, b_out, gain_attn, shift_attn, w_up, b_up, w_down, b_down, gain_ffn, shift_ffn)))
    group_size = math.gcd(SEQS, 8)
    block_count = SEQS // group_size
    input_blocks = layer_in.astype(jnp.float32).reshape(block_count, group_size, SLOTS, D)
    length_blocks = lengths.reshape(block_count, group_size)
    cot_blocks = cotangent.astype(jnp.float32).reshape(block_count, group_size, SLOTS, D)

    def one_block(totals, inputs):
        block_rows, seq_lengths, cot_rows = inputs

        def forward_here(weight_set, input_rows):
            return block_forward(weight_set, input_rows, seq_lengths)
        out_rows, pullback = jax.vjp(forward_here, weights, block_rows)
        row_valid = (lax.broadcasted_iota(jnp.int32, (group_size, SLOTS), 1) < seq_lengths[:, None]).astype(jnp.float32)
        grad_weights, grad_rows = pullback(cot_rows * row_valid[:, :, None])
        totals = jax.tree.map(jnp.add, totals, grad_weights)
        return (totals, (out_rows.astype(jnp.bfloat16), grad_rows.astype(jnp.bfloat16)))
    start_sums = jax.tree.map(jnp.zeros_like, weights)
    totals, (out_blocks, grad_blocks) = lax.scan(one_block, start_sums, (input_blocks, length_blocks, cot_blocks))
    layer_out = out_blocks.reshape(SEQS, SLOTS, D)
    input_grad = grad_blocks.reshape(SEQS, SLOTS, D)
    return (layer_out, input_grad, totals[0], totals[1], totals[2], totals[3], totals[4], totals[5], totals[6], totals[7], totals[8], totals[9], totals[10], totals[11], totals[12], totals[13], totals[14])
```

```python
import functools

import jax
import jax.numpy as jnp
from jax import lax
from jax.experimental import pallas as pl
from jax.experimental.pallas import tpu as pltpu
from jax.sharding import Mesh, PartitionSpec as P

DH = 64
EPSILON = 1e-12
MASKED = -1000000000.0
SWAP = [(0, 1), (1, 0)]
F32 = jnp.float32
BF16 = jnp.bfloat16


def core_swap(array):
    return lax.ppermute(array, "core", SWAP)


def ctx_swap(array):
    return lax.ppermute(array, "ctx", SWAP)


def dot_nt(left, right):
    return lax.dot_general(left, right, (((1,), (1,)), ((), ())), preferred_element_type=F32)


def dot_nn(left, right):
    return lax.dot_general(left, right, (((1,), (0,)), ((), ())), preferred_element_type=F32)


def dot_tn(left, right):
    return lax.dot_general(left, right, (((0,), (0,)), ((), ())), preferred_element_type=F32)


def gather_rows(own):
    near = jnp.concatenate([own, core_swap(own)], axis=0)
    across = ctx_swap(own)
    far = jnp.concatenate([across, core_swap(across)], axis=0)
    return near, far


def reduce_rows(near, far):
    rows = near.shape[0] // 2
    send_far = core_swap(far[rows:].astype(BF16))
    across = ctx_swap((far[:rows] + send_far.astype(F32)).astype(BF16))
    send_near = core_swap(near[rows:].astype(BF16))
    return near[:rows] + send_near.astype(F32) + across.astype(F32)


def lane_masks(width):
    lane = lax.broadcasted_iota(jnp.int32, (1, width), 1)
    return [(lane // DH) == head for head in range(width // DH)]


def attend_kernel(counts, qa, ka, va, qb, kb, vb, oa, ob, probs):
    half = qa.shape[0]
    seq = pl.program_id(0)
    keys = jnp.concatenate([ka[...], kb[...]], axis=0)
    values = jnp.concatenate([va[...], vb[...]], axis=0)
    slot = lax.broadcasted_iota(jnp.int32, (1, 2 * half), 1)
    valid = slot < jnp.where(slot < half, counts[seq, 0], counts[seq, 1] + half)
    masks = lane_masks(keys.shape[1])
    for part, (q_ref, o_ref) in enumerate(((qa, oa), (qb, ob))):
        queries = q_ref[...]
        mixed = None
        for head, mask in enumerate(masks):
            scores = dot_nt(jnp.where(mask, queries, jnp.zeros_like(queries)), keys) * DH ** (-0.5)
            scores = jnp.where(valid, scores, MASKED)
            top = jnp.max(scores, axis=-1, keepdims=True)
            raised = jnp.exp(scores - top)
            low = (raised * (1.0 / jnp.sum(raised, axis=-1, keepdims=True))).astype(BF16)
            probs[0, head, part] = low
            out = dot_nn(low, values)
            mixed = out if mixed is None else jnp.where(mask, out, mixed)
        o_ref[...] = mixed.astype(BF16)


def attend(counts, near, far, seqs, width):
    half = near.shape[0] // seqs
    heads = width // DH
    pairs = heads // 2
    spec = lambda part: pl.BlockSpec(
        (half, 2 * DH), lambda s, p, c, part=part: (s, part * pairs + p)
    )
    out_spec = pl.BlockSpec((half, 2 * DH), lambda s, p, c: (s, p))
    return pl.pallas_call(
        attend_kernel,
        grid_spec=pltpu.PrefetchScalarGridSpec(
            num_scalar_prefetch=1,
            grid=(seqs, pairs),
            in_specs=[spec(0), spec(1), spec(2)] * 2,
            out_specs=[
                out_spec,
                out_spec,
                pl.BlockSpec((1, 2, 2, half, 2 * half), lambda s, p, c: (s, p, 0, 0, 0)),
            ],
        ),
        out_shape=[
            jax.ShapeDtypeStruct((seqs * half, width), BF16),
            jax.ShapeDtypeStruct((seqs * half, width), BF16),
            jax.ShapeDtypeStruct((seqs, heads, 2, half, 2 * half), BF16),
        ],
        cost_estimate=pl.CostEstimate(
            flops=16 * seqs * pairs * half * half * 128, bytes_accessed=8 << 20, transcendentals=4 * half * half * heads
        ),
    )(counts, near, near, near, far, far, far)


def attend_back_kernel(qa, ka, va, ga, qb, kb, vb, gb, probs, dqa, dka, dva, dqb, dkb, dvb):
    half = qa.shape[0]
    keys = jnp.concatenate([ka[...], kb[...]], axis=0)
    values = jnp.concatenate([va[...], vb[...]], axis=0)
    masks = lane_masks(keys.shape[1])
    grad_k = grad_v = None
    for part, (q_ref, g_ref, dq_ref) in enumerate(((qa, ga, dqa), (qb, gb, dqb))):
        queries = q_ref[...]
        grads = g_ref[...]
        dq = dk = dv = None
        for head, mask in enumerate(masks):
            low = probs[0, head, part]
            grad_p = dot_nt(jnp.where(mask, grads, jnp.zeros_like(grads)), values)
            weighted = low.astype(F32) * grad_p
            total = jnp.sum(weighted, axis=-1, keepdims=True)
            grad_s = (weighted - low.astype(F32) * total).astype(BF16)
            dq_h = dot_nn(grad_s, keys)
            dk_h = dot_tn(grad_s, queries)
            dv_h = dot_tn(low, grads)
            dq = dq_h if dq is None else jnp.where(mask, dq_h, dq)
            dk = dk_h if dk is None else jnp.where(mask, dk_h, dk)
            dv = dv_h if dv is None else jnp.where(mask, dv_h, dv)
        dq_ref[...] = (dq * DH ** (-0.5)).astype(BF16)
        grad_k = dk if grad_k is None else grad_k + dk
        grad_v = dv if grad_v is None else grad_v + dv
    grad_k = (grad_k * DH ** (-0.5)).astype(BF16)
    grad_v = grad_v.astype(BF16)
    dka[...] = grad_k[:half]
    dkb[...] = grad_k[half:]
    dva[...] = grad_v[:half]
    dvb[...] = grad_v[half:]


def attend_back(near, far, grad_near, grad_far, probs, seqs, width):
    half = near.shape[0] // seqs
    heads = width // DH
    pairs = heads // 2
    spec = lambda part: pl.BlockSpec((half, 2 * DH), lambda s, p, part=part: (s, part * pairs + p))
    plain = pl.BlockSpec((half, 2 * DH), lambda s, p: (s, p))
    side = jax.ShapeDtypeStruct((seqs * half, width), BF16)
    return pl.pallas_call(
        attend_back_kernel,
        grid=(seqs, pairs),
        in_specs=[spec(0), spec(1), spec(2), plain] * 2
        + [pl.BlockSpec((1, 2, 2, half, 2 * half), lambda s, p: (s, p, 0, 0, 0))],
        out_specs=[plain] * 6,
        out_shape=[side] * 6,
        cost_estimate=pl.CostEstimate(
            flops=40 * seqs * pairs * half * half * 128, bytes_accessed=8 << 20, transcendentals=0
        ),
    )(near, near, near, grad_near, far, far, far, grad_far, probs)


def gather_pack(pack, core):
    mine = lax.dynamic_index_in_dim(pack, core, 0, keepdims=False)
    theirs = core_swap(lax.dynamic_index_in_dim(pack, 1 - core, 0, keepdims=False))
    first = jnp.where(core == 0, mine, theirs)
    second = jnp.where(core == 0, theirs, mine)
    rows, held = mine.shape
    both = jnp.stack([first, second])
    full = lax.all_gather(both, ("fx", "tp"), axis=0, tiled=False)
    groups = full.shape[0]
    tp = lax.axis_size("tp")
    full = full.reshape(groups // tp, tp, 2, rows, held)
    return full.transpose(1, 3, 0, 2, 4).reshape(tp, rows, (groups // tp) * 2 * held)


def scatter_pack(grads, core, ctx):
    tp, rows, width = grads.shape
    fx = lax.axis_size("fx")
    held = width // (2 * fx)
    split = grads.astype(BF16).reshape(tp, rows, fx, 2 * held).transpose(2, 0, 1, 3)
    mine = lax.psum_scatter(
        split.reshape(fx * tp, rows, 2 * held), ("fx", "tp"), scatter_dimension=0, tiled=False
    )
    sides = mine.reshape(rows, 2, held)
    keep = lax.dynamic_index_in_dim(sides, core, 1, keepdims=False)
    recv = core_swap(lax.dynamic_index_in_dim(sides, 1 - core, 1, keepdims=False))
    pair = jnp.stack([jnp.where(core == 0, keep, recv), jnp.where(core == 0, recv, keep)])
    other = ctx_swap(pair)
    return jnp.concatenate([jnp.where(ctx == 0, pair, other), jnp.where(ctx == 0, other, pair)])


def norm_parts(rows):
    mean = jnp.mean(rows, axis=-1, keepdims=True)
    centered = rows - mean
    scale = lax.rsqrt(jnp.mean(centered * centered, axis=-1, keepdims=True) + EPSILON)
    return centered * scale, scale


def norm_back(hat, scale, gain, grads):
    scaled = grads * gain
    grad_rows = scale * (
        scaled
        - jnp.mean(scaled, axis=-1, keepdims=True)
        - hat * jnp.mean(scaled * hat, axis=-1, keepdims=True)
    )
    return grad_rows, jnp.sum(grads * hat, axis=0), jnp.sum(grads, axis=0)


def gelu_parts(inner):
    cumulative = 0.5 * (1.0 + lax.erf(inner * (0.5**0.5)))
    density = jnp.exp(-0.5 * inner * inner) * 0.3989422804014327
    return (inner * cumulative).astype(BF16), (cumulative + inner * density).astype(BF16)


def on_device(
    layer_in, lengths, cotangent, w_query, w_key, w_value, b_query, b_value, w_out, b_out,
    gain_attn, shift_attn, w_up, b_up, w_down, b_down, gain_ffn, shift_ffn,
):
    core, ctx, tp_at = lax.axis_index("core"), lax.axis_index("ctx"), lax.axis_index("tp")
    fs_at = lax.axis_index("fx") * 2 + core
    tp = lax.axis_size("tp")
    fsdp = lax.axis_size("fx") * 2
    seq_count, local_slots, model = layer_in.shape
    held = w_query.shape[0]
    seqs = seq_count // tp
    half = local_slots * tp
    rows = seqs * half
    heads_here = w_query.shape[1] // 4
    units_here = w_up.shape[1] // 4

    def by_sequence(array):
        return lax.all_to_all(array, "tp", 0, 1, tiled=True).reshape(rows, model)

    def by_slot(array):
        return lax.all_to_all(array.reshape(seqs, half, model), "tp", 1, 0, tiled=True)

    own_in = by_sequence(layer_in)
    flat = jnp.concatenate(
        [b_query, b_value, b_up, b_out, gain_attn, shift_attn, b_down, gain_ffn, shift_ffn]
    )
    vectors = lax.all_gather(flat, ("tp", "fx", "core"), axis=0, tiled=False).reshape(tp, fsdp, -1)
    sizes = [b_query.shape[0], b_value.shape[0], b_up.shape[0]]

    def part_vector(start, size):
        whole = vectors[:, :, start : start + size].reshape(tp, 4, fsdp * size // 4)
        return lax.dynamic_index_in_dim(whole, 2 * ctx + core, 1, keepdims=False).reshape(-1).astype(F32)

    def model_vector(index):
        start = sum(sizes) + index * held
        return vectors[0, :, start : start + held].reshape(model).astype(F32)

    bias_q = part_vector(0, sizes[0])
    bias_v = part_vector(sizes[0], sizes[1])
    bias_up = part_vector(sizes[0] + sizes[1], sizes[2])
    bias_out, gain_one, shift_one, bias_down, gain_two, shift_two = (model_vector(i) for i in range(6))
    bias_qkv = jnp.concatenate([bias_q, jnp.zeros_like(bias_q), bias_v])

    def columns(weight, width):
        part = lax.dynamic_slice_in_dim(weight, 2 * ctx * width, 2 * width, 1)
        return part.T.reshape(2, width, held)

    def lines(weight, width):
        return lax.dynamic_slice_in_dim(weight, 2 * ctx * width, 2 * width, 0).reshape(2, width, held)

    pack_qkv = jnp.concatenate([columns(w, heads_here) for w in (w_query, w_key, w_value)], axis=1)
    full_qkv = gather_pack(pack_qkv, core)
    full_qkv = full_qkv.reshape(tp, 3, heads_here, model).transpose(1, 0, 2, 3).reshape(-1, model)
    full_out = gather_pack(lines(w_out, heads_here), core).reshape(-1, model)
    full_up = gather_pack(columns(w_up, units_here), core).reshape(-1, model)
    full_down = gather_pack(lines(w_down, units_here), core).reshape(-1, model)
    width = tp * heads_here

    own_len = lax.dynamic_slice_in_dim(lengths, tp_at * seqs, seqs)
    all_len = jnp.concatenate([own_len, core_swap(own_len)])
    counts = jnp.stack(
        [
            jnp.clip(all_len - ctx * half, 0, half),
            jnp.clip(all_len - (1 - ctx) * half, 0, half),
        ],
        axis=1,
    )

    near_in, far_in = gather_rows(own_in)
    near_qkv = (dot_nt(near_in, full_qkv) + bias_qkv).astype(BF16)
    far_qkv = (dot_nt(far_in, full_qkv) + bias_qkv).astype(BF16)
    near_attn, far_attn, probs = attend(counts, near_qkv, far_qkv, 2 * seqs, width)
    projected = reduce_rows(dot_nn(near_attn, full_out), dot_nn(far_attn, full_out)) + bias_out
    hat_one, scale_one = norm_parts(own_in.astype(F32) + projected)
    normed_one = hat_one * gain_one + shift_one
    near_normed, far_normed = gather_rows(normed_one.astype(BF16))
    near_hidden, near_slope = gelu_parts(dot_nt(near_normed, full_up) + bias_up)
    far_hidden, far_slope = gelu_parts(dot_nt(far_normed, full_up) + bias_up)
    ffn = reduce_rows(dot_nn(near_hidden, full_down), dot_nn(far_hidden, full_down)) + bias_down
    hat_two, scale_two = norm_parts(normed_one + ffn)
    layer_out = by_slot((hat_two * gain_two + shift_two).astype(BF16))

    own_cot = by_sequence(cotangent)
    row_slot = ctx * half + lax.broadcasted_iota(jnp.int32, (seqs, half), 1)
    row_valid = (row_slot < own_len[:, None]).reshape(rows, 1)
    grad_out = jnp.where(row_valid, own_cot.astype(F32), 0.0)
    grad_two, grad_gain_two, grad_shift_two = norm_back(hat_two, scale_two, gain_two, grad_out)
    grad_ffn = grad_two.astype(BF16)
    grad_b_down = jnp.sum(grad_ffn.astype(F32), axis=0)
    near_gffn, far_gffn = gather_rows(grad_ffn)
    near_gpre = (dot_nt(near_gffn, full_down) * near_slope.astype(F32)).astype(BF16)
    far_gpre = (dot_nt(far_gffn, full_down) * far_slope.astype(F32)).astype(BF16)
    grad_down = dot_tn(near_hidden, near_gffn) + dot_tn(far_hidden, far_gffn)
    grad_up = dot_tn(near_gpre, near_normed) + dot_tn(far_gpre, far_normed)
    grad_b_up = jnp.sum(near_gpre.astype(F32), axis=0) + jnp.sum(far_gpre.astype(F32), axis=0)
    grad_normed = reduce_rows(dot_nn(near_gpre, full_up), dot_nn(far_gpre, full_up)) + grad_two
    down_parts = scatter_pack(grad_down.reshape(tp, units_here, model), core, ctx)
    up_parts = scatter_pack(grad_up.reshape(tp, units_here, model), core, ctx)

    grad_one, grad_gain_one, grad_shift_one = norm_back(hat_one, scale_one, gain_one, grad_normed)
    grad_proj = grad_one.astype(BF16)
    grad_b_out = jnp.sum(grad_proj.astype(F32), axis=0)
    near_gproj, far_gproj = gather_rows(grad_proj)
    near_gattn = dot_nt(near_gproj, full_out).astype(BF16)
    far_gattn = dot_nt(far_gproj, full_out).astype(BF16)
    grad_out_w = dot_tn(near_attn, near_gproj) + dot_tn(far_attn, far_gproj)
    dqa, dka, dva, dqb, dkb, dvb = attend_back(
        near_qkv, far_qkv, near_gattn, far_gattn, probs, 2 * seqs, width
    )
    near_dqkv = jnp.concatenate([dqa, dka, dva], axis=1)
    far_dqkv = jnp.concatenate([dqb, dkb, dvb], axis=1)
    input_rows = reduce_rows(dot_nn(near_dqkv, full_qkv), dot_nn(far_dqkv, full_qkv)) + grad_one
    input_grad = by_slot(input_rows.astype(BF16))
    grad_qkv = dot_tn(near_dqkv, near_in) + dot_tn(far_dqkv, far_in)
    grad_b_q = jnp.sum(dqa.astype(F32), axis=0) + jnp.sum(dqb.astype(F32), axis=0)
    grad_b_v = jnp.sum(dva.astype(F32), axis=0) + jnp.sum(dvb.astype(F32), axis=0)

    model_rows = jnp.stack(
        [grad_b_out, grad_gain_one, grad_shift_one, grad_b_down, grad_gain_two, grad_shift_two]
    )
    part_rows = jnp.concatenate(
        [grad_b_up.reshape(tp, -1), grad_b_q.reshape(tp, -1), grad_b_v.reshape(tp, -1)], axis=1
    )
    spare = -part_rows.shape[1] % held
    part_rows = jnp.pad(part_rows, ((0, 0), (0, spare))).reshape(tp, -1, held)
    part_count = part_rows.shape[1]
    vector_rows = jnp.concatenate(
        [
            jnp.broadcast_to(model_rows[None], (tp, 6, model)),
            jnp.tile(part_rows, (1, 1, fsdp)),
        ],
        axis=1,
    )
    pad = -vector_rows.shape[1] % 16
    vector_rows = jnp.pad(vector_rows, ((0, 0), (0, pad), (0, 0)))
    attn_grads = jnp.concatenate(
        [
            grad_qkv.astype(BF16).reshape(3, tp, heads_here, model).transpose(1, 0, 2, 3).reshape(tp, -1, model),
            grad_out_w.astype(BF16).reshape(tp, heads_here, model),
            vector_rows.astype(BF16),
        ],
        axis=1,
    )
    attn_parts = scatter_pack(attn_grads, core, ctx).astype(F32)

    def weight_t(block):
        return attn_parts[:, block * heads_here : (block + 1) * heads_here].reshape(-1, held)

    base = 4 * heads_here
    vector_sums = jnp.sum(attn_parts[:, base : base + 6], axis=0)
    part_all = attn_parts[:, base + 6 : base + 6 + part_count].reshape(4, -1)

    def part_grad(start, size, count):
        whole = part_all[:, start : start + size].reshape(-1)
        return lax.dynamic_slice_in_dim(whole, fs_at * count, count)

    grads = (
        weight_t(0).T,
        weight_t(1).T,
        weight_t(2).T,
        part_grad(units_here, heads_here, sizes[0]),
        part_grad(units_here + heads_here, heads_here, sizes[1]),
        weight_t(3),
        vector_sums[0],
        vector_sums[1],
        vector_sums[2],
        up_parts.astype(F32).reshape(-1, held).T,
        part_grad(0, units_here, sizes[2]),
        down_parts.astype(F32).reshape(-1, held),
        vector_sums[3],
        vector_sums[4],
        vector_sums[5],
    )
    return (layer_out, input_grad) + grads


def solution(mesh):
    fsdp, ctx, tp = (mesh.shape[axis] for axis in ("fsdp", "ctx", "tp"))
    split = Mesh(mesh.devices.reshape(fsdp // 2, 2, ctx, tp), ("fx", "core", "ctx", "tp"))
    fs = ("fx", "core")
    rows = P(fs, ("ctx", "tp"), None)
    wide, tall = P(fs, "tp"), P("tp", fs)
    part, model = P(("tp", "fx", "core")), P(fs)
    weights = (wide, wide, wide, part, part, tall, model, model, model, wide, part, tall, model, model, model)
    return jax.shard_map(
        on_device,
        mesh=split,
        in_specs=(rows, P(fs), rows) + weights,
        out_specs=(rows, rows) + weights,
        check_vma=False,
    )
```

```python
import jax
import jax.numpy as jnp
from jax import lax
from jax.experimental import pallas as pl
from jax.experimental.pallas import tpu as pltpu
from jax.sharding import Mesh, PartitionSpec as P

DH = 64
EPSILON = 1e-12
MASKED = -1000000000.0
SWAP = [(0, 1), (1, 0)]
F32 = jnp.float32
BF16 = jnp.bfloat16


def core_swap(array):
    return lax.ppermute(array, "core", SWAP)


def ctx_swap(array):
    return lax.ppermute(array, "ctx", SWAP)


def dot_nt(left, right):
    return lax.dot_general(left, right, (((1,), (1,)), ((), ())), preferred_element_type=F32)


def dot_nn(left, right):
    return lax.dot_general(left, right, (((1,), (0,)), ((), ())), preferred_element_type=F32)


def dot_tn(left, right):
    return lax.dot_general(left, right, (((0,), (0,)), ((), ())), preferred_element_type=F32)


def gather_rows(own):
    near = jnp.concatenate([own, core_swap(own)], axis=0)
    across = ctx_swap(own)
    far = jnp.concatenate([across, core_swap(across)], axis=0)
    return near, far


def reduce_rows(near, far):
    rows = near.shape[0] // 2
    send_far = core_swap(far[rows:].astype(BF16))
    across = ctx_swap((far[:rows] + send_far.astype(F32)).astype(BF16))
    send_near = core_swap(near[rows:].astype(BF16))
    return near[:rows] + send_near.astype(F32) + across.astype(F32)


def lane_masks(width):
    lane = lax.broadcasted_iota(jnp.int32, (1, width), 1)
    return [(lane // DH) == head for head in range(width // DH)]


def attend_kernel(counts, qa, ka, va, qb, kb, vb, oa, ob, probs):
    half = qa.shape[0]
    seq = pl.program_id(0)
    keys = jnp.concatenate([ka[...], kb[...]], axis=0)
    values = jnp.concatenate([va[...], vb[...]], axis=0)
    slot = lax.broadcasted_iota(jnp.int32, (1, 2 * half), 1)
    valid = slot < jnp.where(slot < half, counts[seq, 0], counts[seq, 1] + half)
    masks = lane_masks(keys.shape[1])
    for part, (q_ref, o_ref) in enumerate(((qa, oa), (qb, ob))):
        queries = q_ref[...]
        mixed = None
        for head, mask in enumerate(masks):
            scores = dot_nt(jnp.where(mask, queries, jnp.zeros_like(queries)), keys) * DH ** (-0.5)
            scores = jnp.where(valid, scores, MASKED)
            top = jnp.max(scores, axis=-1, keepdims=True)
            raised = jnp.exp(scores - top)
            low = (raised * (1.0 / jnp.sum(raised, axis=-1, keepdims=True))).astype(BF16)
            probs[0, head, part] = low
            out = dot_nn(low, values)
            mixed = out if mixed is None else jnp.where(mask, out, mixed)
        o_ref[...] = mixed.astype(BF16)


def attend(counts, near, far, seqs, width):
    half = near.shape[0] // seqs
    heads = width // DH
    pairs = heads // 2
    spec = lambda part: pl.BlockSpec(
        (half, 2 * DH), lambda s, p, c, part=part: (s, part * pairs + p)
    )
    out_spec = pl.BlockSpec((half, 2 * DH), lambda s, p, c: (s, p))
    return pl.pallas_call(
        attend_kernel,
        grid_spec=pltpu.PrefetchScalarGridSpec(
            num_scalar_prefetch=1,
            grid=(seqs, pairs),
            in_specs=[spec(0), spec(1), spec(2)] * 2,
            out_specs=[
                out_spec,
                out_spec,
                pl.BlockSpec((1, 2, 2, half, 2 * half), lambda s, p, c: (s, p, 0, 0, 0)),
            ],
        ),
        out_shape=[
            jax.ShapeDtypeStruct((seqs * half, width), BF16),
            jax.ShapeDtypeStruct((seqs * half, width), BF16),
            jax.ShapeDtypeStruct((seqs, heads, 2, half, 2 * half), BF16),
        ],
        cost_estimate=pl.CostEstimate(
            flops=16 * seqs * pairs * half * half * 128, bytes_accessed=8 << 20, transcendentals=4 * half * half * heads
        ),
    )(counts, near, near, near, far, far, far)


def attend_back_kernel(qa, ka, va, ga, qb, kb, vb, gb, probs, dqa, dka, dva, dqb, dkb, dvb):
    half = qa.shape[0]
    keys = jnp.concatenate([ka[...], kb[...]], axis=0)
    values = jnp.concatenate([va[...], vb[...]], axis=0)
    masks = lane_masks(keys.shape[1])
    grad_k = grad_v = None
    for part, (q_ref, g_ref, dq_ref) in enumerate(((qa, ga, dqa), (qb, gb, dqb))):
        queries = q_ref[...]
        grads = g_ref[...]
        dq = dk = dv = None
        for head, mask in enumerate(masks):
            low = probs[0, head, part]
            grad_p = dot_nt(jnp.where(mask, grads, jnp.zeros_like(grads)), values)
            weighted = low.astype(F32) * grad_p
            total = jnp.sum(weighted, axis=-1, keepdims=True)
            grad_s = (weighted - low.astype(F32) * total).astype(BF16)
            dq_h = dot_nn(grad_s, keys)
            dk_h = dot_tn(grad_s, queries)
            dv_h = dot_tn(low, grads)
            dq = dq_h if dq is None else jnp.where(mask, dq_h, dq)
            dk = dk_h if dk is None else jnp.where(mask, dk_h, dk)
            dv = dv_h if dv is None else jnp.where(mask, dv_h, dv)
        dq_ref[...] = (dq * DH ** (-0.5)).astype(BF16)
        grad_k = dk if grad_k is None else grad_k + dk
        grad_v = dv if grad_v is None else grad_v + dv
    grad_k = (grad_k * DH ** (-0.5)).astype(BF16)
    grad_v = grad_v.astype(BF16)
    dka[...] = grad_k[:half]
    dkb[...] = grad_k[half:]
    dva[...] = grad_v[:half]
    dvb[...] = grad_v[half:]


def attend_back(near, far, grad_near, grad_far, probs, seqs, width):
    half = near.shape[0] // seqs
    heads = width // DH
    pairs = heads // 2
    spec = lambda part: pl.BlockSpec((half, 2 * DH), lambda s, p, part=part: (s, part * pairs + p))
    plain = pl.BlockSpec((half, 2 * DH), lambda s, p: (s, p))
    side = jax.ShapeDtypeStruct((seqs * half, width), BF16)
    return pl.pallas_call(
        attend_back_kernel,
        grid=(seqs, pairs),
        in_specs=[spec(0), spec(1), spec(2), plain] * 2
        + [pl.BlockSpec((1, 2, 2, half, 2 * half), lambda s, p: (s, p, 0, 0, 0))],
        out_specs=[plain] * 6,
        out_shape=[side] * 6,
        cost_estimate=pl.CostEstimate(
            flops=40 * seqs * pairs * half * half * 128, bytes_accessed=8 << 20, transcendentals=0
        ),
    )(near, near, near, grad_near, far, far, far, grad_far, probs)


def by_half(index, own, other, axis):
    return jnp.where(index == 0, jnp.concatenate([own, other], axis), jnp.concatenate([other, own], axis))


def fx_swap(array):
    return lax.ppermute(array, "fx", SWAP)


def after(value, *others):
    return lax.optimization_barrier((value,) + others)[0]


def pack_block(pieces, core):
    mine = jnp.concatenate([own for own, _ in pieces], axis=0)
    theirs = core_swap(jnp.concatenate([other for _, other in pieces], axis=0))
    return by_half(core, mine, theirs, 1)


def gather_tp(block):
    return lax.all_gather(block, "tp", axis=0, tiled=True)


def gather_fx(near, fx):
    groups = lax.axis_size("fx")
    if groups == 2:
        return by_half(fx, near, fx_swap(near), 1)
    return lax.all_gather(near, "fx", axis=0, tiled=False).transpose(1, 0, 2).reshape(near.shape[0], -1)


def scatter_fx(product, fx, held):
    groups = lax.axis_size("fx")
    pair = 2 * held
    if groups == 2:
        sent = fx_swap(product((1 - fx) * pair, pair).astype(BF16))
        return sent, lambda sent: (product(fx * pair, pair) + sent.astype(F32)).astype(BF16)
    whole = product(0, groups * pair).astype(BF16)
    split = whole.reshape(-1, groups, pair).transpose(1, 0, 2)
    return lax.psum_scatter(split, "fx", scatter_dimension=0, tiled=False), lambda summed: summed


def scatter_tp(summed):
    return lax.psum_scatter(summed, "tp", scatter_dimension=0, tiled=True)


def finish_fx(mine, fx, held):
    groups = lax.axis_size("fx")
    pair = 2 * held
    if groups == 2:
        sent = fx_swap(lax.dynamic_slice_in_dim(mine, (1 - fx) * pair, pair, 1))
        keep = lax.dynamic_slice_in_dim(mine, fx * pair, pair, 1)
        return (keep.astype(F32) + sent.astype(F32)).astype(BF16)
    split = mine.reshape(-1, groups, pair).transpose(1, 0, 2)
    return lax.psum_scatter(split, "fx", scatter_dimension=0, tiled=False)


def parts_of(mine, core, ctx, held):
    keep = lax.dynamic_slice_in_dim(mine, core * held, held, 1)
    recv = core_swap(lax.dynamic_slice_in_dim(mine, (1 - core) * held, held, 1))
    both = by_half(core, keep, recv, 0)
    return by_half(ctx, both, ctx_swap(both), 0).reshape(4, -1, held)


def norm_parts(rows):
    mean = jnp.mean(rows, axis=-1, keepdims=True)
    centered = rows - mean
    scale = lax.rsqrt(jnp.mean(centered * centered, axis=-1, keepdims=True) + EPSILON)
    return centered * scale, scale


def norm_back(hat, scale, gain, grads):
    scaled = grads * gain
    grad_rows = scale * (
        scaled
        - jnp.mean(scaled, axis=-1, keepdims=True)
        - hat * jnp.mean(scaled * hat, axis=-1, keepdims=True)
    )
    return grad_rows, jnp.sum(grads * hat, axis=0), jnp.sum(grads, axis=0)


def gelu_parts(inner):
    cumulative = 0.5 * (1.0 + lax.erf(inner * (0.5**0.5)))
    density = jnp.exp(-0.5 * inner * inner) * 0.3989422804014327
    return (inner * cumulative).astype(BF16), (cumulative + inner * density).astype(BF16)


def on_device(
    layer_in, lengths, cotangent, w_query, w_key, w_value, b_query, b_value, w_out, b_out,
    gain_attn, shift_attn, w_up, b_up, w_down, b_down, gain_ffn, shift_ffn,
):
    core, ctx, tp_at = lax.axis_index("core"), lax.axis_index("ctx"), lax.axis_index("tp")
    fx_at = lax.axis_index("fx")
    fs_at = fx_at * 2 + core
    tp = lax.axis_size("tp")
    fsdp = lax.axis_size("fx") * 2
    seq_count, local_slots, model = layer_in.shape
    held = w_query.shape[0]
    seqs = seq_count // tp
    half = local_slots * tp
    rows = seqs * half
    heads_here = w_query.shape[1] // 4
    units_here = w_up.shape[1] // 4

    def by_sequence(array):
        blocks = array.reshape(tp, seqs, local_slots, model)
        return lax.all_to_all(blocks, "tp", 0, 0).transpose(1, 0, 2, 3).reshape(rows, model)

    def by_slot(array):
        blocks = array.reshape(seqs, tp, local_slots, model).transpose(1, 0, 2, 3)
        return lax.all_to_all(blocks, "tp", 0, 0).reshape(seq_count, local_slots, model)

    def parted(weight, width, axis):
        first = 2 * ctx * width
        parts = [
            lax.dynamic_slice_in_dim(weight, first + side * width, width, axis) for side in (core, 1 - core)
        ]
        return tuple(part.T if axis else part for part in parts)

    flats = (b_query, b_value, b_up, b_out, gain_attn, shift_attn, b_down, gain_ffn, shift_ffn)
    flat_rows = 16
    flat_at = lax.broadcasted_iota(jnp.int32, (flat_rows, held), 0)
    flat_block = jnp.zeros((flat_rows, held), BF16)
    for at, flat in enumerate(flats):
        flat_block = jnp.where(flat_at == at, jnp.pad(flat, (0, held - flat.shape[0]))[None], flat_block)
    first_block = pack_block(
        [parted(w, heads_here, 1) for w in (w_query, w_key, w_value)]
        + [parted(w_out, heads_here, 0), (flat_block, flat_block)],
        core,
    )
    up_block = gather_fx(pack_block([parted(w_up, units_here, 1)], core), fx_at)
    down_block = gather_fx(pack_block([parted(w_down, units_here, 0)], core), fx_at)
    first_near = gather_tp(first_block)
    full_up = gather_tp(up_block)
    full_down = gather_tp(down_block)
    own_in = by_sequence(after(layer_in, first_near, up_block, down_block))
    first_pack = gather_fx(first_near, fx_at).reshape(tp, -1, model)
    full_qkv = first_pack[:, : 3 * heads_here].reshape(tp, 3, heads_here, model)
    full_qkv = full_qkv.transpose(1, 0, 2, 3).reshape(-1, model)
    full_out = first_pack[:, 3 * heads_here : 4 * heads_here].reshape(-1, model)
    width = tp * heads_here
    flat_first = 4 * heads_here

    def part_vector(at, size):
        whole = first_pack[:, flat_first + at].reshape(tp, fsdp, held)[:, :, :size].reshape(tp, 4, -1)
        return lax.dynamic_index_in_dim(whole, 2 * ctx + core, 1, keepdims=False).reshape(-1).astype(F32)

    def model_vector(at):
        return first_pack[0, flat_first + at].astype(F32)

    sizes = [b_query.shape[0], b_value.shape[0], b_up.shape[0]]
    bias_q, bias_v, bias_up = (part_vector(at, size) for at, size in enumerate(sizes))
    bias_out, gain_one, shift_one, bias_down, gain_two, shift_two = (model_vector(3 + i) for i in range(6))
    bias_qkv = jnp.concatenate([bias_q, jnp.zeros_like(bias_q), bias_v])

    own_len = lax.dynamic_slice_in_dim(lengths, tp_at * seqs, seqs)
    all_len = jnp.concatenate([own_len, core_swap(own_len)])
    counts = jnp.stack(
        [
            jnp.clip(all_len - ctx * half, 0, half),
            jnp.clip(all_len - (1 - ctx) * half, 0, half),
        ],
        axis=1,
    )

    near_in, far_in = gather_rows(own_in)
    near_qkv = (dot_nt(near_in, full_qkv) + bias_qkv).astype(BF16)
    far_qkv = (dot_nt(far_in, full_qkv) + bias_qkv).astype(BF16)
    near_attn, far_attn, probs = attend(counts, near_qkv, far_qkv, 2 * seqs, width)
    projected = reduce_rows(dot_nn(near_attn, full_out), dot_nn(far_attn, full_out)) + bias_out
    hat_one, scale_one = norm_parts(own_in.astype(F32) + projected)
    hat_one, own_cot = lax.optimization_barrier((hat_one, by_sequence(cotangent)))
    normed_one = hat_one * gain_one + shift_one
    near_normed, far_normed = gather_rows(normed_one.astype(BF16))
    near_hidden, near_slope = gelu_parts(dot_nt(near_normed, full_up) + bias_up)
    far_hidden, far_slope = gelu_parts(dot_nt(far_normed, full_up) + bias_up)
    ffn = reduce_rows(dot_nn(near_hidden, full_down), dot_nn(far_hidden, full_down)) + bias_down
    hat_two, scale_two = norm_parts(normed_one + ffn)
    layer_out = by_slot((hat_two * gain_two + shift_two).astype(BF16))

    row_slot = ctx * half + lax.broadcasted_iota(jnp.int32, (seqs, half), 1)
    row_valid = (row_slot < own_len[:, None]).reshape(rows, 1)
    grad_out = jnp.where(row_valid, own_cot.astype(F32), 0.0)
    grad_two, grad_gain_two, grad_shift_two = norm_back(hat_two, scale_two, gain_two, grad_out)
    grad_ffn = grad_two.astype(BF16)
    grad_b_down = jnp.sum(grad_ffn.astype(F32), axis=0)
    near_gffn, far_gffn = gather_rows(grad_ffn)
    near_gpre = (dot_nt(near_gffn, full_down) * near_slope.astype(F32)).astype(BF16)
    far_gpre = (dot_nt(far_gffn, full_down) * far_slope.astype(F32)).astype(BF16)

    def columns(array, start, size):
        return lax.dynamic_slice_in_dim(array, start, size, 1)

    def product(near_left, far_left, near_right, far_right):
        return lambda start, size: (
            dot_tn(near_left, columns(near_right, start, size)) + dot_tn(far_left, columns(far_right, start, size))
        )

    grad_b_up = jnp.sum(near_gpre.astype(F32), axis=0) + jnp.sum(far_gpre.astype(F32), axis=0)
    down_mine = scatter_tp((dot_tn(near_hidden, near_gffn) + dot_tn(far_hidden, far_gffn)).astype(BF16))
    up_mine = scatter_tp((dot_tn(near_gpre, near_normed) + dot_tn(far_gpre, far_normed)).astype(BF16))
    grad_normed = reduce_rows(dot_nn(near_gpre, full_up), dot_nn(far_gpre, full_up)) + grad_two
    grad_one, grad_gain_one, grad_shift_one = norm_back(hat_one, scale_one, gain_one, grad_normed)
    grad_proj = grad_one.astype(BF16)
    grad_b_out = jnp.sum(grad_proj.astype(F32), axis=0)
    near_gproj, far_gproj = gather_rows(grad_proj)
    near_gattn = dot_nt(near_gproj, full_out).astype(BF16)
    far_gattn = dot_nt(far_gproj, full_out).astype(BF16)
    out_product = product(near_attn, far_attn, near_gproj, far_gproj)
    dqa, dka, dva, dqb, dkb, dvb = attend_back(
        near_qkv, far_qkv, near_gattn, far_gattn, probs, 2 * seqs, width
    )
    dqa, layer_out = lax.optimization_barrier((dqa, layer_out))
    near_dqkv = jnp.concatenate([dqa, dka, dva], axis=1)
    far_dqkv = jnp.concatenate([dqb, dkb, dvb], axis=1)
    qkv_product = product(near_dqkv, far_dqkv, near_in, far_in)
    grad_b_q = jnp.sum(dqa.astype(F32), axis=0) + jnp.sum(dqb.astype(F32), axis=0)
    grad_b_v = jnp.sum(dva.astype(F32), axis=0) + jnp.sum(dvb.astype(F32), axis=0)

    model_rows = jnp.stack(
        [grad_b_out, grad_gain_one, grad_shift_one, grad_b_down, grad_gain_two, grad_shift_two]
    )
    part_rows = jnp.concatenate(
        [grad_b_up.reshape(tp, -1), grad_b_q.reshape(tp, -1), grad_b_v.reshape(tp, -1)], axis=1
    )
    spare = -part_rows.shape[1] % held
    part_rows = jnp.pad(part_rows, ((0, 0), (0, spare))).reshape(tp, -1, held)
    part_count = part_rows.shape[1]
    vector_rows = jnp.concatenate(
        [
            jnp.broadcast_to(model_rows[None], (tp, 6, model)),
            jnp.tile(part_rows, (1, 1, fsdp)),
        ],
        axis=1,
    )
    pad = -vector_rows.shape[1] % 16
    vector_rows = jnp.pad(vector_rows, ((0, 0), (0, pad), (0, 0)))

    def attn_product(start, size):
        grad_qkv = qkv_product(start, size).reshape(3, tp, heads_here, size).transpose(1, 0, 2, 3)
        return jnp.concatenate(
            [
                grad_qkv.reshape(tp, 3 * heads_here, size),
                out_product(start, size).reshape(tp, heads_here, size),
                lax.dynamic_slice_in_dim(vector_rows, start, size, 2),
            ],
            axis=1,
        ).reshape(-1, size)

    attn_sent, attn_add = scatter_fx(attn_product, fx_at, held)
    input_rows = reduce_rows(dot_nn(near_dqkv, full_qkv), dot_nn(far_dqkv, full_qkv)) + grad_one
    input_grad = by_slot(input_rows.astype(BF16))
    attn_sum = attn_add(after(attn_sent, input_rows))
    attn_mine = scatter_tp(attn_sum)
    ffn_mine = finish_fx(after(jnp.concatenate([down_mine, up_mine], axis=0), attn_sum), fx_at, held)
    ffn_parts, attn_parts = (parts_of(mine, core, ctx, held).astype(F32) for mine in (ffn_mine, attn_mine))
    down_parts, up_parts = ffn_parts[:, :units_here], ffn_parts[:, units_here:]

    def weight_t(block):
        return attn_parts[:, block * heads_here : (block + 1) * heads_here].reshape(-1, held)

    base = 4 * heads_here
    vector_sums = jnp.sum(attn_parts[:, base : base + 6], axis=0)
    part_all = attn_parts[:, base + 6 : base + 6 + part_count].reshape(4, -1)

    def part_grad(start, size, count):
        whole = part_all[:, start : start + size].reshape(-1)
        return lax.dynamic_slice_in_dim(whole, fs_at * count, count)

    grads = (
        weight_t(0).T,
        weight_t(1).T,
        weight_t(2).T,
        part_grad(units_here, heads_here, sizes[0]),
        part_grad(units_here + heads_here, heads_here, sizes[1]),
        weight_t(3),
        vector_sums[0],
        vector_sums[1],
        vector_sums[2],
        up_parts.reshape(-1, held).T,
        part_grad(0, units_here, sizes[2]),
        down_parts.reshape(-1, held),
        vector_sums[3],
        vector_sums[4],
        vector_sums[5],
    )
    return (layer_out, input_grad) + grads


def solution(mesh):
    fsdp, ctx, tp = (mesh.shape[axis] for axis in ("fsdp", "ctx", "tp"))
    split = Mesh(mesh.devices.reshape(fsdp // 2, 2, ctx, tp), ("fx", "core", "ctx", "tp"))
    fs = ("fx", "core")
    rows = P(fs, ("ctx", "tp"), None)
    wide, tall = P(fs, "tp"), P("tp", fs)
    part, model = P(("tp", "fx", "core")), P(fs)
    weights = (wide, wide, wide, part, part, tall, model, model, model, wide, part, tall, model, model, model)
    return jax.shard_map(
        on_device,
        mesh=split,
        in_specs=(rows, P(fs), rows) + weights,
        out_specs=(rows, rows) + weights,
        check_vma=False,
    )
```

```python
import jax
import jax.numpy as jnp
from jax import lax
from jax.experimental import pallas as pl
from jax.experimental.pallas import tpu as pltpu
from jax.sharding import Mesh, PartitionSpec as P

DH = 64
EPSILON = 1e-12
MASKED = -1000000000.0
SWAP = [(0, 1), (1, 0)]
F32 = jnp.float32
BF16 = jnp.bfloat16


def core_swap(array):
    return lax.ppermute(array, "core", SWAP)


def ctx_swap(array):
    return lax.ppermute(array, "ctx", SWAP)


def dot_nt(left, right):
    return lax.dot_general(left, right, (((1,), (1,)), ((), ())), preferred_element_type=F32)


def dot_nn(left, right):
    return lax.dot_general(left, right, (((1,), (0,)), ((), ())), preferred_element_type=F32)


def dot_tn(left, right):
    return lax.dot_general(left, right, (((0,), (0,)), ((), ())), preferred_element_type=F32)


def gather_rows(own):
    near = jnp.concatenate([own, core_swap(own)], axis=0)
    across = ctx_swap(own)
    far = jnp.concatenate([across, core_swap(across)], axis=0)
    return near, far


def far_sums(far):
    rows = far.shape[0] // 2
    return (far[:rows] + core_swap(far[rows:].astype(BF16)).astype(F32)).astype(BF16)


def near_sums(near):
    rows = near.shape[0] // 2
    return near[:rows] + core_swap(near[rows:].astype(BF16)).astype(F32)


def reduce_rows(near, far):
    sent = far_sums(far)
    return near_sums(near) + ctx_swap(sent).astype(F32), sent


def lane_masks(width):
    lane = lax.broadcasted_iota(jnp.int32, (1, width), 1)
    return [(lane // DH) == head for head in range(width // DH)]


PAIR = 2 * DH
QUERIES, KEYS, VALUES = (slice(at * PAIR, (at + 1) * PAIR) for at in range(3))


def attend_kernel(counts, slots, qkv_a, qkv_b, oa, ob, probs):
    half = qkv_a.shape[0]
    seq = pl.program_id(0)
    keys = jnp.concatenate([qkv_a[:, KEYS], qkv_b[:, KEYS]], axis=0)
    values = jnp.concatenate([qkv_a[:, VALUES], qkv_b[:, VALUES]], axis=0)
    row = lax.broadcasted_iota(jnp.int32, (1, 2 * half), 1)
    valid = slots[...] < jnp.where(row < half, counts[seq, 0], counts[seq, 1])
    masks = lane_masks(keys.shape[1])
    for part, (qkv_ref, o_ref) in enumerate(((qkv_a, oa), (qkv_b, ob))):
        queries = qkv_ref[:, QUERIES]
        mixed = None
        for head, mask in enumerate(masks):
            scores = dot_nt(jnp.where(mask, queries, jnp.zeros_like(queries)), keys) * DH ** (-0.5)
            scores = jnp.where(valid, scores, MASKED)
            top = jnp.max(scores, axis=-1, keepdims=True)
            raised = jnp.exp(scores - top)
            low = (raised * (1.0 / jnp.sum(raised, axis=-1, keepdims=True))).astype(BF16)
            probs[0, head, part] = low
            out = dot_nn(low, values)
            mixed = out if mixed is None else jnp.where(mask, out, mixed)
        o_ref[...] = mixed.astype(BF16)


def attend(counts, slots, near, far, seqs, width):
    half = near.shape[0] // seqs
    heads = width // DH
    pairs = heads // 2
    spec = pl.BlockSpec((half, 3 * PAIR), lambda s, p, c: (s, p))
    out_spec = pl.BlockSpec((half, 2 * DH), lambda s, p, c: (s, p))
    return pl.pallas_call(
        attend_kernel,
        grid_spec=pltpu.PrefetchScalarGridSpec(
            num_scalar_prefetch=1,
            grid=(seqs, pairs),
            in_specs=[pl.BlockSpec((1, 2 * half), lambda s, p, c: (0, 0)), spec, spec],
            out_specs=[
                out_spec,
                out_spec,
                pl.BlockSpec((1, 2, 2, half, 2 * half), lambda s, p, c: (s, p, 0, 0, 0)),
            ],
        ),
        out_shape=[
            jax.ShapeDtypeStruct((seqs * half, width), BF16),
            jax.ShapeDtypeStruct((seqs * half, width), BF16),
            jax.ShapeDtypeStruct((seqs, heads, 2, half, 2 * half), BF16),
        ],
        cost_estimate=pl.CostEstimate(
            flops=16 * seqs * pairs * half * half * 128, bytes_accessed=8 << 20, transcendentals=4 * half * half * heads
        ),
    )(counts, slots, near, far)


def attend_back_kernel(qkv_a, ga, qkv_b, gb, probs, da, db):
    half = qkv_a.shape[0]
    keys = jnp.concatenate([qkv_a[:, KEYS], qkv_b[:, KEYS]], axis=0)
    values = jnp.concatenate([qkv_a[:, VALUES], qkv_b[:, VALUES]], axis=0)
    masks = lane_masks(keys.shape[1])
    grad_k = grad_v = None
    for part, (qkv_ref, g_ref, d_ref) in enumerate(((qkv_a, ga, da), (qkv_b, gb, db))):
        queries = qkv_ref[:, QUERIES]
        grads = g_ref[...]
        dq = dk = dv = None
        for head, mask in enumerate(masks):
            low = probs[0, head, part]
            grad_p = dot_nt(jnp.where(mask, grads, jnp.zeros_like(grads)), values)
            weighted = low.astype(F32) * grad_p
            total = jnp.sum(weighted, axis=-1, keepdims=True)
            grad_s = (weighted - low.astype(F32) * total).astype(BF16)
            dq_h = dot_nn(grad_s, keys)
            dk_h = dot_tn(grad_s, queries)
            dv_h = dot_tn(low, grads)
            dq = dq_h if dq is None else jnp.where(mask, dq_h, dq)
            dk = dk_h if dk is None else jnp.where(mask, dk_h, dk)
            dv = dv_h if dv is None else jnp.where(mask, dv_h, dv)
        d_ref[:, QUERIES] = (dq * DH ** (-0.5)).astype(BF16)
        grad_k = dk if grad_k is None else grad_k + dk
        grad_v = dv if grad_v is None else grad_v + dv
    grad_k = (grad_k * DH ** (-0.5)).astype(BF16)
    grad_v = grad_v.astype(BF16)
    da[:, KEYS] = grad_k[:half]
    db[:, KEYS] = grad_k[half:]
    da[:, VALUES] = grad_v[:half]
    db[:, VALUES] = grad_v[half:]


def attend_back(near, far, grad_near, grad_far, probs, seqs, width):
    half = near.shape[0] // seqs
    heads = width // DH
    pairs = heads // 2
    spec = pl.BlockSpec((half, 3 * PAIR), lambda s, p: (s, p))
    plain = pl.BlockSpec((half, PAIR), lambda s, p: (s, p))
    side = jax.ShapeDtypeStruct((seqs * half, 3 * width), BF16)
    return pl.pallas_call(
        attend_back_kernel,
        grid=(seqs, pairs),
        in_specs=[spec, plain] * 2
        + [pl.BlockSpec((1, 2, 2, half, 2 * half), lambda s, p: (s, p, 0, 0, 0))],
        out_specs=[spec] * 2,
        out_shape=[side] * 2,
        cost_estimate=pl.CostEstimate(
            flops=40 * seqs * pairs * half * half * 128, bytes_accessed=8 << 20, transcendentals=0
        ),
    )(near, grad_near, far, grad_far, probs)


def by_half(index, own, other, axis):
    return jnp.where(index == 0, jnp.concatenate([own, other], axis), jnp.concatenate([other, own], axis))


def fx_swap(array):
    return lax.ppermute(array, "fx", SWAP)


def after(value, *others):
    return lax.optimization_barrier((value,) + others)[0]


def pack_block(pieces, core):
    mine = jnp.concatenate([own for own, _ in pieces], axis=0)
    theirs = core_swap(jnp.concatenate([other for _, other in pieces], axis=0))
    return by_half(core, mine, theirs, 1)


def tp_turn(array, turn):
    size = lax.axis_size("tp")
    return lax.ppermute(array, "tp", [(at, (at + turn) % size) for at in range(size)]) if turn % size else array


def gather_tp(block):
    return lax.all_gather(block, "tp", axis=0, tiled=True)


def gather_fx(near, fx):
    groups = lax.axis_size("fx")
    if groups == 2:
        return by_half(fx, near, fx_swap(near), 1)
    return lax.all_gather(near, "fx", axis=0, tiled=False).transpose(1, 0, 2).reshape(near.shape[0], -1)


def halves_fx(near):
    rows = near.shape[0] // 2
    return [fx_swap(near[:rows]), fx_swap(near[rows:])] if lax.axis_size("fx") == 2 else []


def join_fx(near, other, fx):
    return by_half(fx, near, jnp.concatenate(other, axis=0), 1) if other else gather_fx(near, fx)


def scatter_fx(product, fx, held):
    groups = lax.axis_size("fx")
    pair = 2 * held
    if groups == 2:
        sent = [fx_swap(turn) for turn in list(product((1 - fx) * pair, pair).astype(BF16))]

        def own(wait):
            return list(product(fx * pair, pair, wait))

        return sent, own
    whole = product(0, groups * pair).astype(BF16)
    sums = [
        lax.psum_scatter(
            turn.reshape(-1, groups, pair).transpose(1, 0, 2), "fx", scatter_dimension=0, tiled=False
        )
        for turn in whole
    ]
    return sums, lambda wait: [jnp.zeros(turn.shape, F32) for turn in sums]


def scatter_tp(summed):
    return lax.psum_scatter(summed, "tp", scatter_dimension=0, tiled=True)


def finish_fx(mine, fx, held):
    groups = lax.axis_size("fx")
    pair = 2 * held
    if groups == 2:
        sent = fx_swap(lax.dynamic_slice_in_dim(mine, (1 - fx) * pair, pair, 1))
        keep = lax.dynamic_slice_in_dim(mine, fx * pair, pair, 1)
        return (keep.astype(F32) + sent.astype(F32)).astype(BF16)
    split = mine.reshape(-1, groups, pair).transpose(1, 0, 2)
    return lax.psum_scatter(split, "fx", scatter_dimension=0, tiled=False)


def parts_of(mine, core, ctx, held):
    keep = lax.dynamic_slice_in_dim(mine, core * held, held, 1)
    recv = core_swap(lax.dynamic_slice_in_dim(mine, (1 - core) * held, held, 1))
    both = by_half(core, keep, recv, 0)
    return by_half(ctx, both, ctx_swap(both), 0).reshape(4, -1, held)


def norm_parts(rows):
    mean = jnp.mean(rows, axis=-1, keepdims=True)
    centered = rows - mean
    scale = lax.rsqrt(jnp.mean(centered * centered, axis=-1, keepdims=True) + EPSILON)
    return centered * scale, scale


def norm_back(hat, scale, gain, grads):
    scaled = grads * gain
    grad_rows = scale * (
        scaled
        - jnp.mean(scaled, axis=-1, keepdims=True)
        - hat * jnp.mean(scaled * hat, axis=-1, keepdims=True)
    )
    return grad_rows, jnp.sum(grads * hat, axis=0), jnp.sum(grads, axis=0)


def gelu_parts(inner):
    cumulative = 0.5 * (1.0 + lax.erf(inner * (0.5**0.5)))
    density = jnp.exp(-0.5 * inner * inner) * 0.3989422804014327
    return (inner * cumulative).astype(BF16), (cumulative + inner * density).astype(BF16)


def on_device(
    layer_in, lengths, cotangent, w_query, w_key, w_value, b_query, b_value, w_out, b_out,
    gain_attn, shift_attn, w_up, b_up, w_down, b_down, gain_ffn, shift_ffn,
):
    core, ctx, tp_at = lax.axis_index("core"), lax.axis_index("ctx"), lax.axis_index("tp")
    fx_at = lax.axis_index("fx")
    fs_at = fx_at * 2 + core
    tp = lax.axis_size("tp")
    fsdp = lax.axis_size("fx") * 2
    seq_count, local_slots, model = layer_in.shape
    held = w_query.shape[0]
    seqs = seq_count // tp
    half = local_slots * tp
    rows = seqs * half
    heads_here = w_query.shape[1] // 4
    units_here = w_up.shape[1] // 4

    def owner(turn):
        return lax.rem(tp_at + turn + tp, tp)

    def by_sequence(array):
        blocks = array.reshape(tp, seqs, local_slots, model)
        turns = [
            tp_turn(lax.dynamic_index_in_dim(blocks, owner(turn), 0, keepdims=False), turn) for turn in range(tp)
        ]
        return jnp.concatenate(turns, axis=1).reshape(rows, model)

    def turns_of(array):
        blocks = array.reshape(seqs, tp, local_slots, model)
        return [tp_turn(blocks[:, turn], -turn) for turn in range(tp)]

    def by_order(turns):
        whole = jnp.zeros((tp,) + turns[0].shape, turns[0].dtype)
        for turn, block in enumerate(turns):
            whole = lax.dynamic_update_index_in_dim(whole, block, owner(turn), 0)
        return whole.reshape(seq_count, local_slots, model)

    def by_turn(array):
        block = lax.broadcasted_iota(jnp.int32, (tp, tp, 1), 0)
        turn = lax.broadcasted_iota(jnp.int32, (tp, tp, 1), 1)
        return jnp.sum(jnp.where(lax.rem(tp_at - turn + tp, tp) == block, array[None], 0.0), axis=1)

    row_at = lax.broadcasted_iota(jnp.int32, (1, half), 1)
    row_slot = lax.rem(tp_at - row_at // local_slots + tp, tp) * local_slots + row_at % local_slots

    def parted(weight, width, axis):
        first = 2 * ctx * width
        parts = [
            lax.dynamic_slice_in_dim(weight, first + side * width, width, axis) for side in (core, 1 - core)
        ]
        return tuple(part.T if axis else part for part in parts)

    flats = (b_query, b_value, b_up, b_out, gain_attn, shift_attn, b_down, gain_ffn, shift_ffn)
    flat_rows = 16
    flat_at = lax.broadcasted_iota(jnp.int32, (flat_rows, held), 0)
    flat_block = jnp.zeros((flat_rows, held), BF16)
    for at, flat in enumerate(flats):
        flat_block = jnp.where(flat_at == at, jnp.pad(flat, (0, held - flat.shape[0]))[None], flat_block)
    first_block = pack_block(
        [parted(w, heads_here, 1) for w in (w_query, w_key, w_value)]
        + [parted(w_out, heads_here, 0), (flat_block, flat_block)],
        core,
    )
    up_block = gather_fx(pack_block([parted(w_up, units_here, 1)], core), fx_at)
    down_block = pack_block([parted(w_down, units_here, 0)], core)
    own_in = by_sequence(after(layer_in, first_block))
    first_turns = [tp_turn(first_block, turn) for turn in range(tp)]
    up_block, down_block, *first_turns[1:] = lax.optimization_barrier([up_block, down_block] + first_turns[1:])
    first_pack = jnp.stack([gather_fx(turn, fx_at) for turn in first_turns])
    down_near = gather_tp(down_block)
    full_up = gather_tp(up_block)
    full_qkv = first_pack[:, : 3 * heads_here].reshape(tp // 2, 2, 3, heads_here, model)
    full_qkv = full_qkv.transpose(0, 2, 1, 3, 4).reshape(-1, model)
    full_out = first_pack[:, 3 * heads_here : 4 * heads_here].reshape(-1, model)
    width = tp * heads_here
    flat_first = 4 * heads_here

    def part_vector(at, size):
        whole = first_pack[:, flat_first + at].reshape(tp, fsdp, held)[:, :, :size].reshape(tp, 4, -1)
        return lax.dynamic_index_in_dim(whole, 2 * ctx + core, 1, keepdims=False).astype(F32)

    def model_vector(at):
        return first_pack[0, flat_first + at].astype(F32)

    sizes = [b_query.shape[0], b_value.shape[0], b_up.shape[0]]
    bias_q, bias_v, bias_up = (part_vector(at, size) for at, size in enumerate(sizes))
    bias_out, gain_one, shift_one, bias_down, gain_two, shift_two = (model_vector(3 + i) for i in range(6))
    bias_up = by_turn(bias_up).reshape(-1)
    bias_qkv = jnp.stack([bias_q, jnp.zeros_like(bias_q), bias_v], axis=1).reshape(tp // 2, 2, 3, heads_here)
    bias_qkv = bias_qkv.transpose(0, 2, 1, 3).reshape(-1)

    own_len = lax.dynamic_slice_in_dim(lengths, tp_at * seqs, seqs)
    all_len = jnp.concatenate([own_len, core_swap(own_len)])
    counts = jnp.stack(
        [
            jnp.clip(all_len - ctx * half, 0, half),
            jnp.clip(all_len - (1 - ctx) * half, 0, half),
        ],
        axis=1,
    )

    near_in, far_in = gather_rows(own_in)
    near_qkv = (dot_nt(near_in, full_qkv) + bias_qkv).astype(BF16)
    far_qkv = (dot_nt(far_in, full_qkv) + bias_qkv).astype(BF16)
    near_attn, far_attn, probs = attend(counts, jnp.tile(row_slot, (1, 2)), near_qkv, far_qkv, 2 * seqs, width)
    projected, _ = reduce_rows(dot_nn(near_attn, full_out), dot_nn(far_attn, full_out))
    projected += bias_out
    hat_one, scale_one = norm_parts(own_in.astype(F32) + projected)
    down_other = halves_fx(down_near)
    hat_one, *down_other[:1] = lax.optimization_barrier([hat_one] + down_other[:1])
    normed_one = hat_one * gain_one + shift_one
    near_normed, far_normed = gather_rows(normed_one.astype(BF16))
    far_normed, *down_other[1:] = lax.optimization_barrier([far_normed] + down_other[1:])
    full_down = join_fx(down_near, down_other, fx_at)
    near_hidden, near_slope = gelu_parts(dot_nt(near_normed, full_up) + bias_up)
    far_hidden, far_slope = gelu_parts(dot_nt(far_normed, full_up) + bias_up)
    ffn, _ = reduce_rows(dot_nn(near_hidden, full_down), dot_nn(far_hidden, full_down))
    ffn += bias_down
    hat_two, scale_two = norm_parts(normed_one + ffn)
    hat_two, own_cot = lax.optimization_barrier((hat_two, by_sequence(cotangent)))
    layer_out = by_order(turns_of((hat_two * gain_two + shift_two).astype(BF16)))

    row_valid = (ctx * half + row_slot < own_len[:, None]).reshape(rows, 1)
    grad_out = jnp.where(row_valid, own_cot.astype(F32), 0.0)
    grad_two, grad_gain_two, grad_shift_two = norm_back(hat_two, scale_two, gain_two, grad_out)
    grad_ffn = grad_two.astype(BF16)
    grad_b_down = jnp.sum(grad_ffn.astype(F32), axis=0)
    near_gffn, far_gffn = gather_rows(grad_ffn)
    near_gpre = (dot_nt(near_gffn, full_down) * near_slope.astype(F32)).astype(BF16)
    far_gpre = (dot_nt(far_gffn, full_down) * far_slope.astype(F32)).astype(BF16)

    def columns(array, start, size):
        return lax.dynamic_slice_in_dim(array, start, size, 1)

    def product(near_left, far_left, near_right, far_right):
        return lambda start, size: (
            dot_tn(near_left, columns(near_right, start, size)) + dot_tn(far_left, columns(far_right, start, size))
        )

    grad_b_up = jnp.sum(near_gpre.astype(F32), axis=0) + jnp.sum(far_gpre.astype(F32), axis=0)
    grad_normed, normed_sent = reduce_rows(dot_nn(near_gpre, full_up), dot_nn(far_gpre, full_up))
    grad_normed += grad_two

    def product_after(near_left, far_left, near_right, far_right, wait):
        near_left, far_left, _ = lax.optimization_barrier((near_left, far_left, wait))
        return (dot_tn(far_left, far_right) + dot_tn(near_left, near_right)).astype(BF16)

    down_mine = scatter_tp(product_after(near_hidden, far_hidden, near_gffn, far_gffn, normed_sent))
    up_mine = scatter_tp(product_after(near_gpre, far_gpre, near_normed, far_normed, normed_sent))
    grad_one, grad_gain_one, grad_shift_one = norm_back(hat_one, scale_one, gain_one, grad_normed)
    grad_proj = grad_one.astype(BF16)
    grad_b_out = jnp.sum(grad_proj.astype(F32), axis=0)
    near_gproj, far_gproj = gather_rows(grad_proj)
    near_gattn = dot_nt(near_gproj, full_out).astype(BF16)
    far_gattn = dot_nt(far_gproj, full_out).astype(BF16)
    out_product = product(near_attn, far_attn, near_gproj, far_gproj)
    near_dqkv, far_dqkv = attend_back(near_qkv, far_qkv, near_gattn, far_gattn, probs, 2 * seqs, width)
    near_dqkv, layer_out = lax.optimization_barrier((near_dqkv, layer_out))
    grad_b_qkv = jnp.sum(near_dqkv.astype(F32), axis=0) + jnp.sum(far_dqkv.astype(F32), axis=0)
    grad_b_qkv = grad_b_qkv.reshape(tp // 2, 3, 2, heads_here)
    grad_b_q, grad_b_v = grad_b_qkv[:, 0], grad_b_qkv[:, 2]

    model_rows = jnp.stack(
        [grad_b_out, grad_gain_one, grad_shift_one, grad_b_down, grad_gain_two, grad_shift_two]
    )
    part_rows = jnp.concatenate(
        [by_turn(grad_b_up.reshape(tp, -1)), grad_b_q.reshape(tp, -1), grad_b_v.reshape(tp, -1)], axis=1
    )
    spare = -part_rows.shape[1] % held
    part_rows = jnp.pad(part_rows, ((0, 0), (0, spare))).reshape(tp, -1, held)
    part_count = part_rows.shape[1]
    vector_rows = jnp.concatenate(
        [
            jnp.broadcast_to(model_rows[None], (tp, 6, model)),
            jnp.tile(part_rows, (1, 1, fsdp)),
        ],
        axis=1,
    )
    pad = -vector_rows.shape[1] % 16
    vector_rows = jnp.pad(vector_rows, ((0, 0), (0, pad), (0, 0)))

    def attn_product(start, size, wait=None):
        left = far_dqkv if wait is None else after(far_dqkv, wait)
        grad_qkv = product(near_dqkv, left, near_in, far_in)(start, size)
        grad_qkv = grad_qkv.reshape(tp // 2, 3, 2, heads_here, size).transpose(0, 2, 1, 3, 4)
        return jnp.concatenate(
            [
                grad_qkv.reshape(tp, 3 * heads_here, size),
                out_product(start, size).reshape(tp, heads_here, size),
                lax.dynamic_slice_in_dim(vector_rows, start, size, 2),
            ],
            axis=1,
        )

    fence = lax.optimization_barrier
    attn_sent, attn_own = scatter_fx(attn_product, fx_at, held)
    input_sent = far_sums(dot_nn(far_dqkv, full_qkv))
    input_near = near_sums(dot_nn(after(near_dqkv, input_sent), full_qkv)) + grad_one
    attn_own = attn_own(input_sent)
    early, late = (2, 1), (3, 0)
    input_across = ctx_swap(input_sent)
    input_across, input_near, attn_own, early_sent = fence(
        (input_across, input_near, attn_own, [attn_sent[turn] for turn in early])
    )
    input_turns = turns_of((input_near + input_across.astype(F32)).astype(BF16))

    def to_owner(turn, sent):
        return tp_turn((attn_own[turn] + sent.astype(F32)).astype(BF16), -turn)

    got_first, got_second = (to_owner(turn, sent) for turn, sent in zip(early, early_sent))
    ffn_both = after(jnp.concatenate([down_mine, up_mine], axis=0), input_across)
    ffn_mine = finish_fx(ffn_both, fx_at, held)
    input_turns, got_first, ffn_mine, late_sent = fence(
        (input_turns, got_first, ffn_mine, [attn_sent[turn] for turn in late])
    )
    got_late = [to_owner(turn, sent) for turn, sent in zip(late, late_sent)]
    ffn_parts = parts_of(ffn_mine, core, ctx, held)
    got_second, got_late, ffn_parts = fence((got_second, got_late, ffn_parts))
    attn_mine = sum(got.astype(F32) for got in [got_first, got_second] + got_late).astype(BF16)
    input_grad = by_order(input_turns)
    ffn_parts, attn_parts = ffn_parts.astype(F32), parts_of(attn_mine, core, ctx, held).astype(F32)
    down_parts, up_parts = ffn_parts[:, :units_here], ffn_parts[:, units_here:]

    def weight_t(block):
        return attn_parts[:, block * heads_here : (block + 1) * heads_here].reshape(-1, held)

    base = 4 * heads_here
    vector_sums = jnp.sum(attn_parts[:, base : base + 6], axis=0)
    part_all = attn_parts[:, base + 6 : base + 6 + part_count].reshape(4, -1)

    def part_grad(start, size, count):
        whole = part_all[:, start : start + size].reshape(-1)
        return lax.dynamic_slice_in_dim(whole, fs_at * count, count)

    grads = (
        weight_t(0).T,
        weight_t(1).T,
        weight_t(2).T,
        part_grad(units_here, heads_here, sizes[0]),
        part_grad(units_here + heads_here, heads_here, sizes[1]),
        weight_t(3),
        vector_sums[0],
        vector_sums[1],
        vector_sums[2],
        up_parts.reshape(-1, held).T,
        part_grad(0, units_here, sizes[2]),
        down_parts.reshape(-1, held),
        vector_sums[3],
        vector_sums[4],
        vector_sums[5],
    )
    return (layer_out, input_grad) + grads


def solution(mesh):
    fsdp, ctx, tp = (mesh.shape[axis] for axis in ("fsdp", "ctx", "tp"))
    split = Mesh(mesh.devices.reshape(fsdp // 2, 2, ctx, tp), ("fx", "core", "ctx", "tp"))
    fs = ("fx", "core")
    rows = P(fs, ("ctx", "tp"), None)
    wide, tall = P(fs, "tp"), P("tp", fs)
    part, model = P(("tp", "fx", "core")), P(fs)
    weights = (wide, wide, wide, part, part, tall, model, model, model, wide, part, tall, model, model, model)
    return jax.shard_map(
        on_device,
        mesh=split,
        in_specs=(rows, P(fs), rows) + weights,
        out_specs=(rows, rows) + weights,
        check_vma=False,
    )
```

```python
import jax
import jax.numpy as jnp
from jax import lax
from jax.experimental import pallas as pl
from jax.experimental.pallas import tpu as pltpu
from jax.sharding import Mesh, PartitionSpec as P

DH = 64
EPSILON = 1e-12
MASKED = -1000000000.0
SWAP = [(0, 1), (1, 0)]
F32 = jnp.float32
BF16 = jnp.bfloat16


def core_swap(array):
    return lax.ppermute(array, "core", SWAP)


def ctx_swap(array):
    return lax.ppermute(array, "ctx", SWAP)


def dot_nt(left, right):
    return lax.dot_general(left, right, (((1,), (1,)), ((), ())), preferred_element_type=F32)


def dot_nn(left, right):
    return lax.dot_general(left, right, (((1,), (0,)), ((), ())), preferred_element_type=F32)


def dot_tn(left, right):
    return lax.dot_general(left, right, (((0,), (0,)), ((), ())), preferred_element_type=F32)


def gather_rows(own, beside=()):
    near = jnp.concatenate([own, core_swap(own)], axis=0)
    across, beside = lax.optimization_barrier((ctx_swap(own), beside))
    far = jnp.concatenate([across, core_swap(across)], axis=0)
    return (near, far, beside) if beside else (near, far)


def far_sums(far):
    rows = far.shape[0] // 2
    return (far[:rows] + core_swap(far[rows:].astype(BF16)).astype(F32)).astype(BF16)


def near_sums(near):
    rows = near.shape[0] // 2
    return near[:rows] + core_swap(near[rows:].astype(BF16)).astype(F32)


def reduce_rows(near, far):
    sent = far_sums(far)
    return near_sums(near) + ctx_swap(sent).astype(F32), sent


def lane_masks(width):
    lane = lax.broadcasted_iota(jnp.int32, (1, width), 1)
    return [(lane // DH) == head for head in range(width // DH)]


PAIR = 2 * DH
QUERIES, KEYS, VALUES = (slice(at * PAIR, (at + 1) * PAIR) for at in range(3))


def attend_kernel(counts, slots, qkv_a, qkv_b, oa, ob, probs):
    half = qkv_a.shape[0]
    seq = pl.program_id(0)
    keys = jnp.concatenate([qkv_a[:, KEYS], qkv_b[:, KEYS]], axis=0)
    values = jnp.concatenate([qkv_a[:, VALUES], qkv_b[:, VALUES]], axis=0)
    row = lax.broadcasted_iota(jnp.int32, (1, 2 * half), 1)
    valid = slots[...] < jnp.where(row < half, counts[seq, 0], counts[seq, 1])
    masks = lane_masks(keys.shape[1])
    for part, (qkv_ref, o_ref) in enumerate(((qkv_a, oa), (qkv_b, ob))):
        queries = qkv_ref[:, QUERIES]
        mixed = None
        for head, mask in enumerate(masks):
            scores = dot_nt(jnp.where(mask, queries, jnp.zeros_like(queries)), keys) * DH ** (-0.5)
            scores = jnp.where(valid, scores, MASKED)
            top = jnp.max(scores, axis=-1, keepdims=True)
            raised = jnp.exp(scores - top)
            low = (raised * (1.0 / jnp.sum(raised, axis=-1, keepdims=True))).astype(BF16)
            probs[0, head, part] = low
            out = dot_nn(low, values)
            mixed = out if mixed is None else jnp.where(mask, out, mixed)
        o_ref[...] = mixed.astype(BF16)


def attend(counts, slots, near, far, seqs, width):
    half = near.shape[0] // seqs
    heads = width // DH
    pairs = heads // 2
    spec = pl.BlockSpec((half, 3 * PAIR), lambda s, p, c: (s, p))
    out_spec = pl.BlockSpec((half, 2 * DH), lambda s, p, c: (s, p))
    return pl.pallas_call(
        attend_kernel,
        grid_spec=pltpu.PrefetchScalarGridSpec(
            num_scalar_prefetch=1,
            grid=(seqs, pairs),
            in_specs=[pl.BlockSpec((1, 2 * half), lambda s, p, c: (0, 0)), spec, spec],
            out_specs=[
                out_spec,
                out_spec,
                pl.BlockSpec((1, 2, 2, half, 2 * half), lambda s, p, c: (s, p, 0, 0, 0)),
            ],
        ),
        out_shape=[
            jax.ShapeDtypeStruct((seqs * half, width), BF16),
            jax.ShapeDtypeStruct((seqs * half, width), BF16),
            jax.ShapeDtypeStruct((seqs, heads, 2, half, 2 * half), BF16),
        ],
        cost_estimate=pl.CostEstimate(
            flops=16 * seqs * pairs * half * half * 128, bytes_accessed=8 << 20, transcendentals=4 * half * half * heads
        ),
    )(counts, slots, near, far)


def attend_back_kernel(qkv_a, ga, qkv_b, gb, probs, da, db, sums):
    half = qkv_a.shape[0]
    keys = jnp.concatenate([qkv_a[:, KEYS], qkv_b[:, KEYS]], axis=0)
    values = jnp.concatenate([qkv_a[:, VALUES], qkv_b[:, VALUES]], axis=0)
    masks = lane_masks(keys.shape[1])
    grad_k = grad_v = None
    for part, (qkv_ref, g_ref, d_ref) in enumerate(((qkv_a, ga, da), (qkv_b, gb, db))):
        queries = qkv_ref[:, QUERIES]
        grads = g_ref[...]
        dq = dk = dv = None
        for head, mask in enumerate(masks):
            low = probs[0, head, part]
            grad_p = dot_nt(jnp.where(mask, grads, jnp.zeros_like(grads)), values)
            weighted = low.astype(F32) * grad_p
            total = jnp.sum(weighted, axis=-1, keepdims=True)
            grad_s = (weighted - low.astype(F32) * total).astype(BF16)
            dq_h = dot_nn(grad_s, keys)
            dk_h = dot_tn(grad_s, queries)
            dv_h = dot_tn(low, grads)
            dq = dq_h if dq is None else jnp.where(mask, dq_h, dq)
            dk = dk_h if dk is None else jnp.where(mask, dk_h, dk)
            dv = dv_h if dv is None else jnp.where(mask, dv_h, dv)
        d_ref[:, QUERIES] = (dq * DH ** (-0.5)).astype(BF16)
        grad_k = dk if grad_k is None else grad_k + dk
        grad_v = dv if grad_v is None else grad_v + dv
    grad_k = (grad_k * DH ** (-0.5)).astype(BF16)
    grad_v = grad_v.astype(BF16)
    da[:, KEYS] = grad_k[:half]
    db[:, KEYS] = grad_k[half:]
    da[:, VALUES] = grad_v[:half]
    db[:, VALUES] = grad_v[half:]
    both = da[...].astype(F32) + db[...].astype(F32)
    sums[0] = jnp.sum(both, axis=0, keepdims=True)


def attend_back(near, far, grad_near, grad_far, probs, seqs, width):
    half = near.shape[0] // seqs
    heads = width // DH
    pairs = heads // 2
    spec = pl.BlockSpec((half, 3 * PAIR), lambda s, p: (s, p))
    plain = pl.BlockSpec((half, PAIR), lambda s, p: (s, p))
    side = jax.ShapeDtypeStruct((seqs * half, 3 * width), BF16)
    return pl.pallas_call(
        attend_back_kernel,
        grid=(seqs, pairs),
        in_specs=[spec, plain] * 2
        + [pl.BlockSpec((1, 2, 2, half, 2 * half), lambda s, p: (s, p, 0, 0, 0))],
        out_specs=[spec] * 2 + [pl.BlockSpec((1, 1, 3 * PAIR), lambda s, p: (s, 0, p))],
        out_shape=[side] * 2 + [jax.ShapeDtypeStruct((seqs, 1, 3 * width), F32)],
        cost_estimate=pl.CostEstimate(
            flops=40 * seqs * pairs * half * half * 128, bytes_accessed=8 << 20, transcendentals=0
        ),
    )(near, grad_near, far, grad_far, probs)


def by_half(index, own, other, axis):
    return jnp.where(index == 0, jnp.concatenate([own, other], axis), jnp.concatenate([other, own], axis))


def fx_swap(array):
    return lax.ppermute(array, "fx", SWAP)


def after(value, *others):
    return lax.optimization_barrier((value,) + others)[0]


def pack_block(pieces, core):
    mine = jnp.concatenate([own for own, _ in pieces], axis=0)
    theirs = core_swap(jnp.concatenate([other for _, other in pieces], axis=0))
    return by_half(core, mine, theirs, 1)


def tp_turn(array, turn):
    size = lax.axis_size("tp")
    return lax.ppermute(array, "tp", [(at, (at + turn) % size) for at in range(size)]) if turn % size else array


def gather_tp(block):
    return lax.all_gather(block, "tp", axis=0, tiled=True)


def gather_fx(near, fx):
    groups = lax.axis_size("fx")
    if groups == 2:
        return by_half(fx, near, fx_swap(near), 1)
    return lax.all_gather(near, "fx", axis=0, tiled=False).transpose(1, 0, 2).reshape(near.shape[0], -1)


def halves_fx(near):
    rows = near.shape[0] // 2
    return [fx_swap(near[:rows]), fx_swap(near[rows:])] if lax.axis_size("fx") == 2 else []


def join_fx(near, other, fx):
    return by_half(fx, near, jnp.concatenate(other, axis=0), 1) if other else gather_fx(near, fx)


def scatter_fx(product, fx, held):
    groups = lax.axis_size("fx")
    pair = 2 * held
    if groups == 2:
        sends = list(product((1 - fx) * pair, pair).astype(BF16))
        sent = [fx_swap(turn) for turn in sends]

        def own():
            return list(product(fx * pair, pair, sends))

        return sent, own
    whole = product(0, groups * pair).astype(BF16)
    sums = [
        lax.psum_scatter(
            turn.reshape(-1, groups, pair).transpose(1, 0, 2), "fx", scatter_dimension=0, tiled=False
        )
        for turn in whole
    ]
    return sums, lambda: [jnp.zeros(turn.shape, F32) for turn in sums]


def scatter_tp(summed):
    return lax.psum_scatter(summed, "tp", scatter_dimension=0, tiled=True)


def finish_fx(mine, fx, held):
    groups = lax.axis_size("fx")
    pair = 2 * held
    if groups == 2:
        sent = fx_swap(lax.dynamic_slice_in_dim(mine, (1 - fx) * pair, pair, 1))
        keep = lax.dynamic_slice_in_dim(mine, fx * pair, pair, 1)
        return (keep.astype(F32) + sent.astype(F32)).astype(BF16)
    split = mine.reshape(-1, groups, pair).transpose(1, 0, 2)
    return lax.psum_scatter(split, "fx", scatter_dimension=0, tiled=False)


def parts_of(mine, core, ctx, held):
    keep = lax.dynamic_slice_in_dim(mine, core * held, held, 1)
    recv = core_swap(lax.dynamic_slice_in_dim(mine, (1 - core) * held, held, 1))
    both = by_half(core, keep, recv, 0)
    return by_half(ctx, both, ctx_swap(both), 0).reshape(4, -1, held)


def norm_parts(rows):
    mean = jnp.mean(rows, axis=-1, keepdims=True)
    centered = rows - mean
    scale = lax.rsqrt(jnp.mean(centered * centered, axis=-1, keepdims=True) + EPSILON)
    return centered * scale, scale


def norm_back(hat, scale, gain, grads):
    scaled = grads * gain
    grad_rows = scale * (
        scaled
        - jnp.mean(scaled, axis=-1, keepdims=True)
        - hat * jnp.mean(scaled * hat, axis=-1, keepdims=True)
    )
    hat, grads, _ = lax.optimization_barrier((hat, grads, grad_rows))
    return grad_rows, jnp.sum(grads * hat, axis=0), jnp.sum(grads, axis=0)


def gelu_parts(inner):
    cumulative = 0.5 * (1.0 + lax.erf(inner * (0.5**0.5)))
    density = jnp.exp(-0.5 * inner * inner) * 0.3989422804014327
    return (inner * cumulative).astype(BF16), (cumulative + inner * density).astype(BF16)


def on_device(
    layer_in, lengths, cotangent, w_query, w_key, w_value, b_query, b_value, w_out, b_out,
    gain_attn, shift_attn, w_up, b_up, w_down, b_down, gain_ffn, shift_ffn,
):
    core, ctx, tp_at = lax.axis_index("core"), lax.axis_index("ctx"), lax.axis_index("tp")
    fx_at = lax.axis_index("fx")
    fs_at = fx_at * 2 + core
    tp = lax.axis_size("tp")
    fsdp = lax.axis_size("fx") * 2
    fence = lax.optimization_barrier
    seq_count, local_slots, model = layer_in.shape
    held = w_query.shape[0]
    seqs = seq_count // tp
    half = local_slots * tp
    rows = seqs * half
    heads_here = w_query.shape[1] // 4
    units_here = w_up.shape[1] // 4

    def owner(turn):
        return lax.rem(tp_at + turn + tp, tp)

    def by_sequence(array):
        blocks = array.reshape(tp, seqs, local_slots, model)
        turns = [
            tp_turn(lax.dynamic_index_in_dim(blocks, owner(turn), 0, keepdims=False), turn) for turn in range(tp)
        ]
        return jnp.concatenate(turns, axis=1).reshape(rows, model)

    def turns_of(array):
        blocks = array.reshape(seqs, tp, local_slots, model)
        return [tp_turn(blocks[:, turn], -turn) for turn in range(tp)]

    def by_order(turns):
        whole = jnp.zeros((tp,) + turns[0].shape, turns[0].dtype)
        for turn, block in enumerate(turns):
            whole = lax.dynamic_update_index_in_dim(whole, block, owner(turn), 0)
        return whole.reshape(seq_count, local_slots, model)

    def by_turn(array):
        block = lax.broadcasted_iota(jnp.int32, (tp, tp, 1), 0)
        turn = lax.broadcasted_iota(jnp.int32, (tp, tp, 1), 1)
        return jnp.sum(jnp.where(lax.rem(tp_at - turn + tp, tp) == block, array[None], 0.0), axis=1)

    row_at = lax.broadcasted_iota(jnp.int32, (1, half), 1)
    row_slot = lax.rem(tp_at - row_at // local_slots + tp, tp) * local_slots + row_at % local_slots

    def parted(weight, width, axis):
        first = 2 * ctx * width
        parts = [
            lax.dynamic_slice_in_dim(weight, first + side * width, width, axis) for side in (core, 1 - core)
        ]
        return tuple(part.T if axis else part for part in parts)

    flats = (b_query, b_value, b_up, b_out, gain_attn, shift_attn, b_down, gain_ffn, shift_ffn)
    flat_rows = 16
    flat_at = lax.broadcasted_iota(jnp.int32, (flat_rows, held), 0)
    flat_block = jnp.zeros((flat_rows, held), BF16)
    for at, flat in enumerate(flats):
        flat_block = jnp.where(flat_at == at, jnp.pad(flat, (0, held - flat.shape[0]))[None], flat_block)
    first_block = pack_block(
        [parted(w, heads_here, 1) for w in (w_query, w_key, w_value)]
        + [parted(w_out, heads_here, 0), (flat_block, flat_block)],
        core,
    )
    up_block = gather_fx(pack_block([parted(w_up, units_here, 1)], core), fx_at)
    down_block = pack_block([parted(w_down, units_here, 0)], core)
    own_in = by_sequence(after(layer_in, first_block))
    first_turns = [tp_turn(first_block, turn) for turn in range(tp)]
    up_block, down_block, *first_turns[1:] = lax.optimization_barrier([up_block, down_block] + first_turns[1:])
    first_pack = jnp.stack([gather_fx(turn, fx_at) for turn in first_turns])
    down_near = gather_tp(down_block)
    full_up = gather_tp(up_block)
    full_qkv = first_pack[:, : 3 * heads_here].reshape(tp // 2, 2, 3, heads_here, model)
    full_qkv = full_qkv.transpose(0, 2, 1, 3, 4).reshape(-1, model)
    full_out = first_pack[:, 3 * heads_here : 4 * heads_here].reshape(-1, model)
    width = tp * heads_here
    flat_first = 4 * heads_here

    def part_vector(at, size):
        whole = first_pack[:, flat_first + at].reshape(tp, fsdp, held)[:, :, :size].reshape(tp, 4, -1)
        return lax.dynamic_index_in_dim(whole, 2 * ctx + core, 1, keepdims=False).astype(F32)

    def model_vector(at):
        return first_pack[0, flat_first + at].astype(F32)

    sizes = [b_query.shape[0], b_value.shape[0], b_up.shape[0]]
    bias_q, bias_v, bias_up = (part_vector(at, size) for at, size in enumerate(sizes))
    bias_out, gain_one, shift_one, bias_down, gain_two, shift_two = (model_vector(3 + i) for i in range(6))
    bias_up = by_turn(bias_up).reshape(-1)
    bias_qkv = jnp.stack([bias_q, jnp.zeros_like(bias_q), bias_v], axis=1).reshape(tp // 2, 2, 3, heads_here)
    bias_qkv = bias_qkv.transpose(0, 2, 1, 3).reshape(-1)

    own_len = lax.dynamic_slice_in_dim(lengths, tp_at * seqs, seqs)
    all_len = jnp.concatenate([own_len, core_swap(own_len)])
    counts = jnp.stack(
        [
            jnp.clip(all_len - ctx * half, 0, half),
            jnp.clip(all_len - (1 - ctx) * half, 0, half),
        ],
        axis=1,
    )

    near_in, far_in = gather_rows(own_in)
    near_qkv = (dot_nt(near_in, full_qkv) + bias_qkv).astype(BF16)
    far_qkv = (dot_nt(far_in, full_qkv) + bias_qkv).astype(BF16)
    near_attn, far_attn, probs = attend(counts, jnp.tile(row_slot, (1, 2)), near_qkv, far_qkv, 2 * seqs, width)
    far_attn, down_near = fence((far_attn, down_near))
    projected, _ = reduce_rows(dot_nn(near_attn, full_out), dot_nn(far_attn, full_out))
    projected += bias_out
    hat_one, scale_one = norm_parts(own_in.astype(F32) + projected)
    down_other = halves_fx(down_near)
    hat_one, *down_other[:1] = lax.optimization_barrier([hat_one] + down_other[:1])
    normed_one = hat_one * gain_one + shift_one
    near_normed, far_normed = gather_rows(normed_one.astype(BF16))
    far_normed, *down_other[1:] = lax.optimization_barrier([far_normed] + down_other[1:])
    full_down = join_fx(down_near, down_other, fx_at)
    near_hidden, near_slope = gelu_parts(dot_nt(near_normed, full_up) + bias_up)
    far_hidden, far_slope = gelu_parts(dot_nt(far_normed, full_up) + bias_up)
    ffn, _ = reduce_rows(dot_nn(near_hidden, full_down), dot_nn(far_hidden, full_down))
    ffn += bias_down
    hat_two, scale_two = norm_parts(normed_one + ffn)
    hat_two, own_cot = lax.optimization_barrier((hat_two, by_sequence(cotangent)))
    layer_rows = (hat_two * gain_two + shift_two).astype(BF16)

    row_valid = (ctx * half + row_slot < own_len[:, None]).reshape(rows, 1)
    grad_out = jnp.where(row_valid, own_cot.astype(F32), 0.0)
    grad_two, grad_gain_two, grad_shift_two = norm_back(hat_two, scale_two, gain_two, grad_out)
    grad_ffn = grad_two.astype(BF16)
    grad_b_down = jnp.sum(fence(grad_ffn).astype(F32), axis=0)
    near_gffn, far_gffn, layer_turns = gather_rows(grad_ffn, turns_of(layer_rows))
    near_gpre = (dot_nt(near_gffn, full_down) * near_slope.astype(F32)).astype(BF16)
    far_gpre = (dot_nt(far_gffn, full_down) * far_slope.astype(F32)).astype(BF16)

    def columns(array, start, size):
        return lax.dynamic_slice_in_dim(array, start, size, 1)

    def product(near_left, far_left, near_right, far_right):
        return lambda start, size: (
            dot_tn(near_left, columns(near_right, start, size)) + dot_tn(far_left, columns(far_right, start, size))
        )

    grad_b_up = jnp.sum(near_gpre.astype(F32), axis=0) + jnp.sum(far_gpre.astype(F32), axis=0)

    def product_after(near_left, far_left, near_right, far_right, wait):
        near_left, far_left, _ = fence((near_left, far_left, wait))
        return (dot_tn(far_left, far_right) + dot_tn(near_left, near_right)).astype(BF16)

    normed_sent = far_sums(dot_nn(far_gpre, full_up))
    normed_across = ctx_swap(normed_sent)
    normed_near = near_sums(dot_nn(after(near_gpre, normed_sent), full_up)) + grad_two
    grad_down = product_after(near_hidden, far_hidden, near_gffn, far_gffn, normed_sent)

    groups, pair = fsdp // 2, 2 * held

    def up_product(start, size, wait):
        near_left, far_left, _ = fence((near_gpre, far_gpre, wait))
        return product(near_left, far_left, near_normed, far_normed)(start, size)

    up_sends = []
    if groups == 2:
        up_sends = list(up_product((1 - fx_at) * pair, pair, normed_sent).astype(BF16).reshape(2, -1, pair))
    normed_across, normed_near, grad_down, up_sends = fence((normed_across, normed_near, grad_down, up_sends))
    up_got = [fx_swap(half) for half in up_sends]
    down_mine = scatter_tp(grad_down)
    grad_normed = normed_near + normed_across.astype(F32)
    grad_one, grad_gain_one, grad_shift_one = norm_back(hat_one, scale_one, gain_one, grad_normed)
    grad_proj = grad_one.astype(BF16)
    grad_b_out = jnp.sum(fence(grad_proj).astype(F32), axis=0)
    up_own = up_product(fx_at * pair, pair, grad_proj) if groups == 2 else up_product(0, model, grad_proj)
    near_gproj, far_gproj, (up_own, up_got[:1]) = gather_rows(grad_proj, (up_own, up_got[:1]))
    near_gattn = dot_nt(near_gproj, full_out).astype(BF16)
    far_gattn = dot_nt(far_gproj, full_out).astype(BF16)
    out_product = product(near_attn, far_attn, near_gproj, far_gproj)
    out_early = []
    if groups == 2:
        out_early = [out_product((1 - fx_at) * pair, pair).astype(BF16), out_product(fx_at * pair, pair)]
        near_gattn, far_gattn, out_early = fence((near_gattn, far_gattn, out_early))
    near_dqkv, far_dqkv, bias_sums = attend_back(near_qkv, far_qkv, near_gattn, far_gattn, probs, 2 * seqs, width)
    far_dqkv, up_got = fence((far_dqkv, up_got))
    input_sent = far_sums(dot_nn(far_dqkv, full_qkv))
    if groups == 2:
        up_sum = (up_own + jnp.concatenate(up_got, axis=0).astype(F32)).astype(BF16)
        input_sent, down_mine, up_sum = fence((input_sent, down_mine, up_sum))
        up_mine = scatter_tp(up_sum)
    else:
        up_mine = finish_fx(scatter_tp(up_own.astype(BF16)), fx_at, held)
    bias_sums = after(bias_sums, input_sent)
    grad_b_up = after(grad_b_up, input_sent)
    grad_b_qkv = jnp.sum(bias_sums, axis=0).reshape(tp // 2, 3, 2, heads_here)
    grad_b_q, grad_b_v = grad_b_qkv[:, 0], grad_b_qkv[:, 2]

    model_rows = jnp.stack(
        [grad_b_out, grad_gain_one, grad_shift_one, grad_b_down, grad_gain_two, grad_shift_two]
    )
    part_rows = jnp.concatenate(
        [by_turn(grad_b_up.reshape(tp, -1)), grad_b_q.reshape(tp, -1), grad_b_v.reshape(tp, -1)], axis=1
    )
    spare = -part_rows.shape[1] % held
    part_rows = jnp.pad(part_rows, ((0, 0), (0, spare))).reshape(tp, -1, held)
    part_count = part_rows.shape[1]
    vector_rows = jnp.concatenate(
        [
            jnp.broadcast_to(model_rows[None], (tp, 6, model)),
            jnp.tile(part_rows, (1, 1, fsdp)),
        ],
        axis=1,
    )
    pad = -vector_rows.shape[1] % 16
    vector_rows = jnp.pad(vector_rows, ((0, 0), (0, pad), (0, 0)))

    def attn_product(start, size, wait=None):
        left = after(far_dqkv, *([input_sent] if wait is None else wait))
        grad_qkv = product(near_dqkv, left, near_in, far_in)(start, size)
        grad_qkv = grad_qkv.reshape(tp // 2, 3, 2, heads_here, size).transpose(0, 2, 1, 3, 4)
        early = wait is None and groups == 2
        kind = BF16 if early else F32
        grad_out_w = out_early[0 if early else 1] if groups == 2 else out_product(start, size)
        return jnp.concatenate(
            [
                grad_qkv.reshape(tp, 3 * heads_here, size).astype(kind),
                grad_out_w.reshape(tp, heads_here, size).astype(kind),
                lax.dynamic_slice_in_dim(vector_rows, start, size, 2).astype(kind),
            ],
            axis=1,
        )

    attn_sent, attn_own = scatter_fx(attn_product, fx_at, held)
    input_near = near_sums(dot_nn(after(near_dqkv, input_sent), full_qkv)) + grad_one
    attn_own = attn_own()
    early, late = (2, 1), (3, 0)
    input_across = ctx_swap(input_sent)
    input_across, input_near, attn_own, early_sent, up_mine = fence(
        (input_across, input_near, attn_own, [attn_sent[turn] for turn in early], up_mine)
    )
    down_mine = finish_fx(after(down_mine, input_across), fx_at, held)
    input_turns = turns_of((input_near + input_across.astype(F32)).astype(BF16))

    def to_owner(turn, sent):
        return tp_turn((attn_own[turn] + sent.astype(F32)).astype(BF16), -turn)

    got_first, got_second = (to_owner(turn, sent) for turn, sent in zip(early, early_sent))
    input_turns, got_first, down_mine, late_sent = fence(
        (input_turns, got_first, down_mine, [attn_sent[turn] for turn in late])
    )
    ffn_mine = jnp.concatenate([down_mine, up_mine], axis=0)
    got_late = [to_owner(turn, sent) for turn, sent in zip(late, late_sent)]
    ffn_parts = parts_of(ffn_mine, core, ctx, held)
    got_second, got_late, ffn_parts = fence((got_second, got_late, ffn_parts))
    attn_mine = sum(got.astype(F32) for got in [got_first, got_second] + got_late).astype(BF16)
    input_grad = by_order(input_turns)
    layer_out = by_order([after(block, input_sent) for block in layer_turns])
    ffn_parts, attn_parts = ffn_parts.astype(F32), parts_of(attn_mine, core, ctx, held).astype(F32)
    down_parts, up_parts = ffn_parts[:, :units_here], ffn_parts[:, units_here:]

    def weight_t(block):
        return attn_parts[:, block * heads_here : (block + 1) * heads_here].reshape(-1, held)

    base = 4 * heads_here
    vector_sums = jnp.sum(attn_parts[:, base : base + 6], axis=0)
    part_all = attn_parts[:, base + 6 : base + 6 + part_count].reshape(4, -1)

    def part_grad(start, size, count):
        whole = part_all[:, start : start + size].reshape(-1)
        return lax.dynamic_slice_in_dim(whole, fs_at * count, count)

    grads = (
        weight_t(0).T,
        weight_t(1).T,
        weight_t(2).T,
        part_grad(units_here, heads_here, sizes[0]),
        part_grad(units_here + heads_here, heads_here, sizes[1]),
        weight_t(3),
        vector_sums[0],
        vector_sums[1],
        vector_sums[2],
        up_parts.reshape(-1, held).T,
        part_grad(0, units_here, sizes[2]),
        down_parts.reshape(-1, held),
        vector_sums[3],
        vector_sums[4],
        vector_sums[5],
    )
    return (layer_out, input_grad) + grads


def solution(mesh):
    fsdp, ctx, tp = (mesh.shape[axis] for axis in ("fsdp", "ctx", "tp"))
    split = Mesh(mesh.devices.reshape(fsdp // 2, 2, ctx, tp), ("fx", "core", "ctx", "tp"))
    fs = ("fx", "core")
    rows = P(fs, ("ctx", "tp"), None)
    wide, tall = P(fs, "tp"), P("tp", fs)
    part, model = P(("tp", "fx", "core")), P(fs)
    weights = (wide, wide, wide, part, part, tall, model, model, model, wide, part, tall, model, model, model)
    return jax.shard_map(
        on_device,
        mesh=split,
        in_specs=(rows, P(fs), rows) + weights,
        out_specs=(rows, rows) + weights,
        check_vma=False,
    )
```

```python
import jax
import jax.numpy as jnp
from jax import lax
from jax.experimental import pallas as pl
from jax.experimental.pallas import tpu as pltpu
from jax.sharding import Mesh, PartitionSpec as P

DH = 64
EPSILON = 1e-12
MASKED = -1000000000.0
SWAP = [(0, 1), (1, 0)]
F32 = jnp.float32
BF16 = jnp.bfloat16


def core_swap(array):
    return lax.ppermute(array, "core", SWAP)


def ctx_swap(array):
    return lax.ppermute(array, "ctx", SWAP)


def dot_nt(left, right):
    return lax.dot_general(left, right, (((1,), (1,)), ((), ())), preferred_element_type=F32)


def dot_nn(left, right):
    return lax.dot_general(left, right, (((1,), (0,)), ((), ())), preferred_element_type=F32)


def dot_tn(left, right):
    return lax.dot_general(left, right, (((0,), (0,)), ((), ())), preferred_element_type=F32)


def gather_rows(own, beside=()):
    near = jnp.concatenate([own, core_swap(own)], axis=0)
    across, beside = lax.optimization_barrier((ctx_swap(own), beside))
    far = jnp.concatenate([across, core_swap(across)], axis=0)
    return (near, far, beside) if beside else (near, far)


def far_sums(far):
    rows = far.shape[0] // 2
    return (far[:rows] + core_swap(far[rows:].astype(BF16)).astype(F32)).astype(BF16)


def near_sums(near):
    rows = near.shape[0] // 2
    return near[:rows] + core_swap(near[rows:].astype(BF16)).astype(F32)


def reduce_rows(near, far):
    sent = far_sums(far)
    return near_sums(near) + ctx_swap(sent).astype(F32), sent


def lane_masks(width):
    lane = lax.broadcasted_iota(jnp.int32, (1, width), 1)
    return [(lane // DH) == head for head in range(width // DH)]


PAIR = 2 * DH
QUERIES, KEYS, VALUES = (slice(at * PAIR, (at + 1) * PAIR) for at in range(3))


def attend_kernel(counts, slots, qkv_a, qkv_b, oa, ob, probs):
    half = qkv_a.shape[0]
    seq = pl.program_id(0)
    keys = jnp.concatenate([qkv_a[:, KEYS], qkv_b[:, KEYS]], axis=0)
    values = jnp.concatenate([qkv_a[:, VALUES], qkv_b[:, VALUES]], axis=0)
    row = lax.broadcasted_iota(jnp.int32, (1, 2 * half), 1)
    valid = slots[...] < jnp.where(row < half, counts[seq, 0], counts[seq, 1])
    masks = lane_masks(keys.shape[1])
    for part, (qkv_ref, o_ref) in enumerate(((qkv_a, oa), (qkv_b, ob))):
        queries = qkv_ref[:, QUERIES]
        mixed = None
        for head, mask in enumerate(masks):
            scores = dot_nt(jnp.where(mask, queries, jnp.zeros_like(queries)), keys) * DH ** (-0.5)
            scores = jnp.where(valid, scores, MASKED)
            top = jnp.max(scores, axis=-1, keepdims=True)
            raised = jnp.exp(scores - top)
            low = (raised * (1.0 / jnp.sum(raised, axis=-1, keepdims=True))).astype(BF16)
            probs[0, head, part] = low
            out = dot_nn(low, values)
            mixed = out if mixed is None else jnp.where(mask, out, mixed)
        o_ref[...] = mixed.astype(BF16)


def attend(counts, slots, near, far, seqs, width):
    half = near.shape[0] // seqs
    heads = width // DH
    pairs = heads // 2
    spec = pl.BlockSpec((half, 3 * PAIR), lambda s, p, c: (s, p))
    out_spec = pl.BlockSpec((half, 2 * DH), lambda s, p, c: (s, p))
    return pl.pallas_call(
        attend_kernel,
        grid_spec=pltpu.PrefetchScalarGridSpec(
            num_scalar_prefetch=1,
            grid=(seqs, pairs),
            in_specs=[pl.BlockSpec((1, 2 * half), lambda s, p, c: (0, 0)), spec, spec],
            out_specs=[
                out_spec,
                out_spec,
                pl.BlockSpec((1, 2, 2, half, 2 * half), lambda s, p, c: (s, p, 0, 0, 0)),
            ],
        ),
        out_shape=[
            jax.ShapeDtypeStruct((seqs * half, width), BF16),
            jax.ShapeDtypeStruct((seqs * half, width), BF16),
            jax.ShapeDtypeStruct((seqs, heads, 2, half, 2 * half), BF16),
        ],
        cost_estimate=pl.CostEstimate(
            flops=16 * seqs * pairs * half * half * 128, bytes_accessed=8 << 20, transcendentals=4 * half * half * heads
        ),
    )(counts, slots, near, far)


def attend_back_kernel(qkv_a, ga, qkv_b, gb, probs, da, db, sums):
    half = qkv_a.shape[0]
    keys = jnp.concatenate([qkv_a[:, KEYS], qkv_b[:, KEYS]], axis=0)
    values = jnp.concatenate([qkv_a[:, VALUES], qkv_b[:, VALUES]], axis=0)
    masks = lane_masks(keys.shape[1])
    grad_k = grad_v = None
    for part, (qkv_ref, g_ref, d_ref) in enumerate(((qkv_a, ga, da), (qkv_b, gb, db))):
        queries = qkv_ref[:, QUERIES]
        grads = g_ref[...]
        dq = dk = dv = None
        for head, mask in enumerate(masks):
            low = probs[0, head, part]
            grad_p = dot_nt(jnp.where(mask, grads, jnp.zeros_like(grads)), values)
            weighted = low.astype(F32) * grad_p
            total = jnp.sum(weighted, axis=-1, keepdims=True)
            grad_s = (weighted - low.astype(F32) * total).astype(BF16)
            dq_h = dot_nn(grad_s, keys)
            dk_h = dot_tn(grad_s, queries)
            dv_h = dot_tn(low, grads)
            dq = dq_h if dq is None else jnp.where(mask, dq_h, dq)
            dk = dk_h if dk is None else jnp.where(mask, dk_h, dk)
            dv = dv_h if dv is None else jnp.where(mask, dv_h, dv)
        d_ref[:, QUERIES] = (dq * DH ** (-0.5)).astype(BF16)
        grad_k = dk if grad_k is None else grad_k + dk
        grad_v = dv if grad_v is None else grad_v + dv
    grad_k = (grad_k * DH ** (-0.5)).astype(BF16)
    grad_v = grad_v.astype(BF16)
    da[:, KEYS] = grad_k[:half]
    db[:, KEYS] = grad_k[half:]
    da[:, VALUES] = grad_v[:half]
    db[:, VALUES] = grad_v[half:]
    both = da[...].astype(F32) + db[...].astype(F32)
    sums[0] = jnp.sum(both, axis=0, keepdims=True)


def attend_back(near, far, grad_near, grad_far, probs, seqs, width):
    half = near.shape[0] // seqs
    heads = width // DH
    pairs = heads // 2
    spec = pl.BlockSpec((half, 3 * PAIR), lambda s, p: (s, p))
    plain = pl.BlockSpec((half, PAIR), lambda s, p: (s, p))
    side = jax.ShapeDtypeStruct((seqs * half, 3 * width), BF16)
    return pl.pallas_call(
        attend_back_kernel,
        grid=(seqs, pairs),
        in_specs=[spec, plain] * 2
        + [pl.BlockSpec((1, 2, 2, half, 2 * half), lambda s, p: (s, p, 0, 0, 0))],
        out_specs=[spec] * 2 + [pl.BlockSpec((1, 1, 3 * PAIR), lambda s, p: (s, 0, p))],
        out_shape=[side] * 2 + [jax.ShapeDtypeStruct((seqs, 1, 3 * width), F32)],
        cost_estimate=pl.CostEstimate(
            flops=40 * seqs * pairs * half * half * 128, bytes_accessed=8 << 20, transcendentals=0
        ),
    )(near, grad_near, far, grad_far, probs)


def by_half(index, own, other, axis):
    return jnp.where(index == 0, jnp.concatenate([own, other], axis), jnp.concatenate([other, own], axis))


def fx_swap(array):
    return lax.ppermute(array, "fx", SWAP)


def after(value, *others):
    return lax.optimization_barrier((value,) + others)[0]


def pack_block(pieces, core):
    mine = jnp.concatenate([own for own, _ in pieces], axis=0)
    theirs = core_swap(jnp.concatenate([other for _, other in pieces], axis=0))
    return by_half(core, mine, theirs, 1)


def tp_turn(array, turn):
    size = lax.axis_size("tp")
    return lax.ppermute(array, "tp", [(at, (at + turn) % size) for at in range(size)]) if turn % size else array


def gather_tp(block):
    return lax.all_gather(block, "tp", axis=0, tiled=True)


def gather_fx(near, fx):
    groups = lax.axis_size("fx")
    if groups == 2:
        return by_half(fx, near, fx_swap(near), 1)
    return lax.all_gather(near, "fx", axis=0, tiled=False).transpose(1, 0, 2).reshape(near.shape[0], -1)


def halves_fx(near):
    rows = near.shape[0] // 2
    return [fx_swap(near[:rows]), fx_swap(near[rows:])] if lax.axis_size("fx") == 2 else []


def join_fx(near, other, fx):
    return by_half(fx, near, jnp.concatenate(other, axis=0), 1) if other else gather_fx(near, fx)


def scatter_fx(product, fx, held):
    groups = lax.axis_size("fx")
    pair = 2 * held
    if groups == 2:
        sends = list(product((1 - fx) * pair, pair).astype(BF16))
        sent = [fx_swap(turn) for turn in sends]

        def own():
            return list(product(fx * pair, pair, sends))

        return sent, own
    whole = product(0, groups * pair).astype(BF16)
    sums = [
        lax.psum_scatter(
            turn.reshape(-1, groups, pair).transpose(1, 0, 2), "fx", scatter_dimension=0, tiled=False
        )
        for turn in whole
    ]
    return sums, lambda: [jnp.zeros(turn.shape, F32) for turn in sums]


def scatter_tp(summed):
    return lax.psum_scatter(summed, "tp", scatter_dimension=0, tiled=True)


def finish_fx(mine, fx, held):
    groups = lax.axis_size("fx")
    pair = 2 * held
    if groups == 2:
        sent = fx_swap(lax.dynamic_slice_in_dim(mine, (1 - fx) * pair, pair, 1))
        keep = lax.dynamic_slice_in_dim(mine, fx * pair, pair, 1)
        return (keep.astype(F32) + sent.astype(F32)).astype(BF16)
    split = mine.reshape(-1, groups, pair).transpose(1, 0, 2)
    return lax.psum_scatter(split, "fx", scatter_dimension=0, tiled=False)


def parts_of(mine, core, ctx, held):
    keep = lax.dynamic_slice_in_dim(mine, core * held, held, 1)
    recv = core_swap(lax.dynamic_slice_in_dim(mine, (1 - core) * held, held, 1))
    both = by_half(core, keep, recv, 0)
    return by_half(ctx, both, ctx_swap(both), 0).reshape(4, -1, held)


def norm_parts(rows):
    mean = jnp.mean(rows, axis=-1, keepdims=True)
    centered = rows - mean
    scale = lax.rsqrt(jnp.mean(centered * centered, axis=-1, keepdims=True) + EPSILON)
    return centered * scale, scale


def norm_back(hat, scale, gain, grads):
    scaled = grads * gain
    grad_rows = scale * (
        scaled
        - jnp.mean(scaled, axis=-1, keepdims=True)
        - hat * jnp.mean(scaled * hat, axis=-1, keepdims=True)
    )
    hat, grads, _ = lax.optimization_barrier((hat, grads, grad_rows))
    return grad_rows, jnp.sum(grads * hat, axis=0), jnp.sum(grads, axis=0)


def gelu_parts(inner):
    cumulative = 0.5 * (1.0 + lax.erf(inner * (0.5**0.5)))
    density = jnp.exp(-0.5 * inner * inner) * 0.3989422804014327
    return (inner * cumulative).astype(BF16), (cumulative + inner * density).astype(BF16)


def on_device(
    layer_in, lengths, cotangent, w_query, w_key, w_value, b_query, b_value, w_out, b_out,
    gain_attn, shift_attn, w_up, b_up, w_down, b_down, gain_ffn, shift_ffn,
):
    core, ctx, tp_at = lax.axis_index("core"), lax.axis_index("ctx"), lax.axis_index("tp")
    fx_at = lax.axis_index("fx")
    fs_at = fx_at * 2 + core
    tp = lax.axis_size("tp")
    fsdp = lax.axis_size("fx") * 2
    fence = lax.optimization_barrier
    seq_count, local_slots, model = layer_in.shape
    held = w_query.shape[0]
    seqs = seq_count // tp
    half = local_slots * tp
    rows = seqs * half
    heads_here = w_query.shape[1] // 4
    units_here = w_up.shape[1] // 4

    def owner(turn):
        return lax.rem(tp_at + turn + tp, tp)

    def by_sequence(array):
        blocks = array.reshape(tp, seqs, local_slots, model)
        turns = [
            tp_turn(lax.dynamic_index_in_dim(blocks, owner(turn), 0, keepdims=False), turn) for turn in range(tp)
        ]
        return jnp.concatenate(turns, axis=1).reshape(rows, model)

    def turns_of(array):
        blocks = array.reshape(seqs, tp, local_slots, model)
        return [tp_turn(blocks[:, turn], -turn) for turn in range(tp)]

    def by_order(turns):
        whole = jnp.zeros((tp,) + turns[0].shape, turns[0].dtype)
        for turn, block in enumerate(turns):
            whole = lax.dynamic_update_index_in_dim(whole, block, owner(turn), 0)
        return whole.reshape(seq_count, local_slots, model)

    def by_turn(array):
        block = lax.broadcasted_iota(jnp.int32, (tp, tp, 1), 0)
        turn = lax.broadcasted_iota(jnp.int32, (tp, tp, 1), 1)
        return jnp.sum(jnp.where(lax.rem(tp_at - turn + tp, tp) == block, array[None], 0.0), axis=1)

    row_at = lax.broadcasted_iota(jnp.int32, (1, half), 1)
    row_slot = lax.rem(tp_at - row_at // local_slots + tp, tp) * local_slots + row_at % local_slots

    def parted(weight, width, axis):
        first = 2 * ctx * width
        parts = [
            lax.dynamic_slice_in_dim(weight, first + side * width, width, axis) for side in (core, 1 - core)
        ]
        return tuple(part.T if axis else part for part in parts)

    flats = (b_query, b_value, b_up, b_out, gain_attn, shift_attn, b_down, gain_ffn, shift_ffn)
    flat_rows = 16
    flat_at = lax.broadcasted_iota(jnp.int32, (flat_rows, held), 0)
    flat_block = jnp.zeros((flat_rows, held), BF16)
    for at, flat in enumerate(flats):
        flat_block = jnp.where(flat_at == at, jnp.pad(flat, (0, held - flat.shape[0]))[None], flat_block)
    first_block = pack_block(
        [parted(w, heads_here, 1) for w in (w_query, w_key, w_value)]
        + [parted(w_out, heads_here, 0), (flat_block, flat_block)],
        core,
    )
    cut = units_here // 2
    up_pair = pack_block([parted(w_up, units_here, 1)], core)
    up_block = gather_fx(up_pair[:cut], fx_at)
    down_block = pack_block([parted(w_down, units_here, 0)], core)
    down_block = jnp.concatenate([down_block, up_pair[cut:]], axis=0)
    own_in = by_sequence(after(layer_in, first_block))
    first_turns = [tp_turn(first_block, turn) for turn in range(tp)]
    up_block, down_block, *first_turns[1:] = lax.optimization_barrier([up_block, down_block] + first_turns[1:])
    first_pack = jnp.stack([gather_fx(turn, fx_at) for turn in first_turns])
    both_near = gather_tp(down_block).reshape(tp, units_here + cut, -1)
    up_first = gather_tp(up_block).reshape(tp, cut, model)
    full_qkv = first_pack[:, : 3 * heads_here].reshape(tp // 2, 2, 3, heads_here, model)
    full_qkv = full_qkv.transpose(0, 2, 1, 3, 4).reshape(-1, model)
    full_out = first_pack[:, 3 * heads_here : 4 * heads_here].reshape(-1, model)
    width = tp * heads_here
    flat_first = 4 * heads_here

    def part_vector(at, size):
        whole = first_pack[:, flat_first + at].reshape(tp, fsdp, held)[:, :, :size].reshape(tp, 4, -1)
        return lax.dynamic_index_in_dim(whole, 2 * ctx + core, 1, keepdims=False).astype(F32)

    def model_vector(at):
        return first_pack[0, flat_first + at].astype(F32)

    sizes = [b_query.shape[0], b_value.shape[0], b_up.shape[0]]
    bias_q, bias_v, bias_up = (part_vector(at, size) for at, size in enumerate(sizes))
    bias_out, gain_one, shift_one, bias_down, gain_two, shift_two = (model_vector(3 + i) for i in range(6))
    bias_up = by_turn(bias_up).reshape(-1)
    bias_qkv = jnp.stack([bias_q, jnp.zeros_like(bias_q), bias_v], axis=1).reshape(tp // 2, 2, 3, heads_here)
    bias_qkv = bias_qkv.transpose(0, 2, 1, 3).reshape(-1)

    own_len = lax.dynamic_slice_in_dim(lengths, tp_at * seqs, seqs)
    all_len = jnp.concatenate([own_len, core_swap(own_len)])
    counts = jnp.stack(
        [
            jnp.clip(all_len - ctx * half, 0, half),
            jnp.clip(all_len - (1 - ctx) * half, 0, half),
        ],
        axis=1,
    )

    near_in, far_in = gather_rows(own_in)
    near_qkv = (dot_nt(near_in, full_qkv) + bias_qkv).astype(BF16)
    far_qkv = (dot_nt(far_in, full_qkv) + bias_qkv).astype(BF16)
    near_attn, far_attn, probs = attend(counts, jnp.tile(row_slot, (1, 2)), near_qkv, far_qkv, 2 * seqs, width)
    near_attn, both_near = fence((near_attn, both_near))
    down_near = both_near[:, :units_here].reshape(tp * units_here, -1)
    up_near = both_near[:, units_here:].reshape(tp * cut, -1)
    projected, _ = reduce_rows(dot_nn(near_attn, full_out), dot_nn(far_attn, full_out))
    projected += bias_out
    hat_one, scale_one = norm_parts(own_in.astype(F32) + projected)
    up_second = [gather_fx(up_near, fx_at)] if fsdp != 4 else [fx_swap(up_near)]
    down_other = halves_fx(down_near)
    hat_one, up_second = fence((hat_one, up_second))
    up_second = by_half(fx_at, up_near, up_second[0], 1) if fsdp == 4 else up_second[0]
    full_up = jnp.concatenate([up_first, up_second.reshape(tp, cut, model)], axis=1).reshape(-1, model)
    normed_one = hat_one * gain_one + shift_one
    near_normed, far_normed, (down_other[:1], _) = gather_rows(normed_one.astype(BF16), (down_other[:1], hat_one))
    near_normed, *down_other[1:] = fence([near_normed] + down_other[1:])
    near_hidden, near_slope = gelu_parts(dot_nt(near_normed, full_up) + bias_up)
    far_hidden, far_slope = gelu_parts(dot_nt(far_normed, full_up) + bias_up)
    full_down = join_fx(down_near, down_other, fx_at)
    ffn, _ = reduce_rows(dot_nn(near_hidden, full_down), dot_nn(far_hidden, full_down))
    ffn += bias_down
    hat_two, scale_two = norm_parts(normed_one + ffn)
    hat_two, own_cot = lax.optimization_barrier((hat_two, by_sequence(cotangent)))
    layer_rows = (hat_two * gain_two + shift_two).astype(BF16)

    row_valid = (ctx * half + row_slot < own_len[:, None]).reshape(rows, 1)
    grad_out = jnp.where(row_valid, own_cot.astype(F32), 0.0)
    grad_two, grad_gain_two, grad_shift_two = norm_back(hat_two, scale_two, gain_two, grad_out)
    grad_ffn = grad_two.astype(BF16)
    grad_b_down = jnp.sum(fence(grad_ffn).astype(F32), axis=0)
    near_gffn, far_gffn, layer_turns = gather_rows(grad_ffn, turns_of(layer_rows))
    near_gpre = (dot_nt(near_gffn, full_down) * near_slope.astype(F32)).astype(BF16)
    far_gpre = (dot_nt(far_gffn, full_down) * far_slope.astype(F32)).astype(BF16)

    def columns(array, start, size):
        return lax.dynamic_slice_in_dim(array, start, size, 1)

    def product(near_left, far_left, near_right, far_right):
        return lambda start, size: (
            dot_tn(near_left, columns(near_right, start, size)) + dot_tn(far_left, columns(far_right, start, size))
        )

    grad_b_up = jnp.sum(near_gpre.astype(F32), axis=0) + jnp.sum(far_gpre.astype(F32), axis=0)

    def product_after(near_left, far_left, near_right, far_right, wait):
        near_left, far_left, _ = fence((near_left, far_left, wait))
        return (dot_tn(far_left, far_right) + dot_tn(near_left, near_right)).astype(BF16)

    normed_sent = far_sums(dot_nn(far_gpre, full_up))
    normed_across = ctx_swap(normed_sent)
    normed_near = near_sums(dot_nn(after(near_gpre, normed_sent), full_up)) + grad_two
    grad_down = product_after(near_hidden, far_hidden, near_gffn, far_gffn, normed_sent)

    groups, pair = fsdp // 2, 2 * held

    def up_product(start, size, wait):
        near_left, far_left, _ = fence((near_gpre, far_gpre, wait))
        return product(near_left, far_left, near_normed, far_normed)(start, size)

    up_sends = []
    if groups == 2:
        up_sends = list(up_product((1 - fx_at) * pair, pair, normed_sent).astype(BF16).reshape(2, -1, pair))
    normed_across, normed_near, grad_down, up_sends = fence((normed_across, normed_near, grad_down, up_sends))
    up_got = [fx_swap(half) for half in up_sends]
    down_mine = scatter_tp(grad_down)
    grad_normed = normed_near + normed_across.astype(F32)
    grad_one, grad_gain_one, grad_shift_one = norm_back(hat_one, scale_one, gain_one, grad_normed)
    grad_proj = grad_one.astype(BF16)
    grad_b_out = jnp.sum(fence(grad_proj).astype(F32), axis=0)
    up_own = up_product(fx_at * pair, pair, grad_proj) if groups == 2 else up_product(0, model, grad_proj)
    near_gproj, far_gproj, (up_own, up_got[:1]) = gather_rows(grad_proj, (up_own, up_got[:1]))
    near_gattn = dot_nt(near_gproj, full_out).astype(BF16)
    far_gattn = dot_nt(far_gproj, full_out).astype(BF16)
    out_product = product(near_attn, far_attn, near_gproj, far_gproj)
    out_early = []
    if groups == 2:
        out_early = [out_product((1 - fx_at) * pair, pair).astype(BF16), out_product(fx_at * pair, pair)]
        near_gattn, far_gattn, out_early = fence((near_gattn, far_gattn, out_early))
    near_dqkv, far_dqkv, bias_sums = attend_back(near_qkv, far_qkv, near_gattn, far_gattn, probs, 2 * seqs, width)
    far_dqkv, up_got = fence((far_dqkv, up_got))
    input_sent = far_sums(dot_nn(far_dqkv, full_qkv))
    if groups == 2:
        up_sum = (up_own + jnp.concatenate(up_got, axis=0).astype(F32)).astype(BF16)
        input_sent, down_mine, up_sum = fence((input_sent, down_mine, up_sum))
        up_mine = scatter_tp(up_sum)
    else:
        up_mine = finish_fx(scatter_tp(up_own.astype(BF16)), fx_at, held)
    bias_sums = after(bias_sums, input_sent)
    grad_b_up = after(grad_b_up, input_sent)
    grad_b_qkv = jnp.sum(bias_sums, axis=0).reshape(tp // 2, 3, 2, heads_here)
    grad_b_q, grad_b_v = grad_b_qkv[:, 0], grad_b_qkv[:, 2]

    model_rows = jnp.stack(
        [grad_b_out, grad_gain_one, grad_shift_one, grad_b_down, grad_gain_two, grad_shift_two]
    )
    part_rows = jnp.concatenate(
        [by_turn(grad_b_up.reshape(tp, -1)), grad_b_q.reshape(tp, -1), grad_b_v.reshape(tp, -1)], axis=1
    )
    spare = -part_rows.shape[1] % held
    part_rows = jnp.pad(part_rows, ((0, 0), (0, spare))).reshape(tp, -1, held)
    part_count = part_rows.shape[1]
    vector_rows = jnp.concatenate(
        [
            jnp.broadcast_to(model_rows[None], (tp, 6, model)),
            jnp.tile(part_rows, (1, 1, fsdp)),
        ],
        axis=1,
    )
    pad = -vector_rows.shape[1] % 16
    vector_rows = jnp.pad(vector_rows, ((0, 0), (0, pad), (0, 0)))

    def attn_product(start, size, wait=None):
        left = after(far_dqkv, *([input_sent] if wait is None else wait))
        grad_qkv = product(near_dqkv, left, near_in, far_in)(start, size)
        grad_qkv = grad_qkv.reshape(tp // 2, 3, 2, heads_here, size).transpose(0, 2, 1, 3, 4)
        early = wait is None and groups == 2
        kind = BF16 if early else F32
        grad_out_w = out_early[0 if early else 1] if groups == 2 else out_product(start, size)
        return jnp.concatenate(
            [
                grad_qkv.reshape(tp, 3 * heads_here, size).astype(kind),
                grad_out_w.reshape(tp, heads_here, size).astype(kind),
                lax.dynamic_slice_in_dim(vector_rows, start, size, 2).astype(kind),
            ],
            axis=1,
        )

    attn_sent, attn_own = scatter_fx(attn_product, fx_at, held)
    input_near = near_sums(dot_nn(after(near_dqkv, input_sent), full_qkv)) + grad_one
    attn_own = attn_own()
    early, late = (2, 1), (3, 0)
    input_across = ctx_swap(input_sent)
    input_across, input_near, attn_own, early_sent, up_mine = fence(
        (input_across, input_near, attn_own, [attn_sent[turn] for turn in early], up_mine)
    )
    down_mine = finish_fx(after(down_mine, input_across), fx_at, held)
    input_turns = turns_of((input_near + input_across.astype(F32)).astype(BF16))

    def to_owner(turn, sent):
        return tp_turn((attn_own[turn] + sent.astype(F32)).astype(BF16), -turn)

    got_first, got_second = (to_owner(turn, sent) for turn, sent in zip(early, early_sent))
    input_turns, got_first, down_mine, late_sent = fence(
        (input_turns, got_first, down_mine, [attn_sent[turn] for turn in late])
    )
    ffn_mine = jnp.concatenate([down_mine, up_mine], axis=0)
    got_late = [to_owner(turn, sent) for turn, sent in zip(late, late_sent)]
    ffn_parts = parts_of(ffn_mine, core, ctx, held)
    got_second, got_late, ffn_parts = fence((got_second, got_late, ffn_parts))
    attn_mine = sum(got.astype(F32) for got in [got_first, got_second] + got_late).astype(BF16)
    input_grad = by_order(input_turns)
    layer_out = by_order([after(block, input_sent) for block in layer_turns])
    ffn_parts, attn_parts = ffn_parts.astype(F32), parts_of(attn_mine, core, ctx, held).astype(F32)
    down_parts, up_parts = ffn_parts[:, :units_here], ffn_parts[:, units_here:]

    def weight_t(block):
        return attn_parts[:, block * heads_here : (block + 1) * heads_here].reshape(-1, held)

    base = 4 * heads_here
    vector_sums = jnp.sum(attn_parts[:, base : base + 6], axis=0)
    part_all = attn_parts[:, base + 6 : base + 6 + part_count].reshape(4, -1)

    part_here = lax.dynamic_index_in_dim(part_all, lax.rem(fs_at, 4), 0, keepdims=False)

    def part_grad(start, size, count):
        if count == size:
            return part_here[start : start + size]
        whole = part_all[:, start : start + size].reshape(-1)
        return lax.dynamic_slice_in_dim(whole, fs_at * count, count)

    grads = (
        weight_t(0).T,
        weight_t(1).T,
        weight_t(2).T,
        part_grad(units_here, heads_here, sizes[0]),
        part_grad(units_here + heads_here, heads_here, sizes[1]),
        weight_t(3),
        vector_sums[0],
        vector_sums[1],
        vector_sums[2],
        up_parts.reshape(-1, held).T,
        part_grad(0, units_here, sizes[2]),
        down_parts.reshape(-1, held),
        vector_sums[3],
        vector_sums[4],
        vector_sums[5],
    )
    return (layer_out, input_grad) + grads


def solution(mesh):
    fsdp, ctx, tp = (mesh.shape[axis] for axis in ("fsdp", "ctx", "tp"))
    split = Mesh(mesh.devices.reshape(fsdp // 2, 2, ctx, tp), ("fx", "core", "ctx", "tp"))
    fs = ("fx", "core")
    rows = P(fs, ("ctx", "tp"), None)
    wide, tall = P(fs, "tp"), P("tp", fs)
    part, model = P(("tp", "fx", "core")), P(fs)
    weights = (wide, wide, wide, part, part, tall, model, model, model, wide, part, tall, model, model, model)
    return jax.shard_map(
        on_device,
        mesh=split,
        in_specs=(rows, P(fs), rows) + weights,
        out_specs=(rows, rows) + weights,
        check_vma=False,
    )
```

```python
import jax
import jax.numpy as jnp
from jax import lax
from jax.experimental import pallas as pl
from jax.experimental.pallas import tpu as pltpu
from jax.sharding import Mesh, PartitionSpec as P

DH = 64
EPSILON = 1e-12
MASKED = -1000000000.0
SWAP = [(0, 1), (1, 0)]
F32 = jnp.float32
BF16 = jnp.bfloat16


def core_swap(array):
    return lax.ppermute(array, "core", SWAP)


def ctx_swap(array):
    return lax.ppermute(array, "ctx", SWAP)


def dot_nt(left, right):
    return lax.dot_general(left, right, (((1,), (1,)), ((), ())), preferred_element_type=F32)


def dot_nn(left, right):
    return lax.dot_general(left, right, (((1,), (0,)), ((), ())), preferred_element_type=F32)


def dot_tn(left, right):
    return lax.dot_general(left, right, (((0,), (0,)), ((), ())), preferred_element_type=F32)


def gather_rows(own, beside=()):
    near = jnp.concatenate([own, core_swap(own)], axis=0)
    across, beside = lax.optimization_barrier((ctx_swap(own), beside))
    far = jnp.concatenate([across, core_swap(across)], axis=0)
    return (near, far, beside) if beside else (near, far)


def far_sums(far):
    rows = far.shape[0] // 2
    return (far[:rows] + core_swap(far[rows:].astype(BF16)).astype(F32)).astype(BF16)


def near_sums(near):
    rows = near.shape[0] // 2
    return near[:rows] + core_swap(near[rows:].astype(BF16)).astype(F32)


def reduce_rows(near, far):
    sent = far_sums(far)
    return near_sums(near) + ctx_swap(sent).astype(F32), sent


def lane_masks(width):
    lane = lax.broadcasted_iota(jnp.int32, (1, width), 1)
    return [(lane // DH) == head for head in range(width // DH)]


PAIR = 2 * DH
QUERIES, KEYS, VALUES = (slice(at * PAIR, (at + 1) * PAIR) for at in range(3))


def attend_kernel(counts, slots, qkv_a, qkv_b, oa, ob, probs):
    half = qkv_a.shape[0]
    seq = pl.program_id(0)
    keys = jnp.concatenate([qkv_a[:, KEYS], qkv_b[:, KEYS]], axis=0)
    values = jnp.concatenate([qkv_a[:, VALUES], qkv_b[:, VALUES]], axis=0)
    row = lax.broadcasted_iota(jnp.int32, (1, 2 * half), 1)
    valid = slots[...] < jnp.where(row < half, counts[seq, 0], counts[seq, 1])
    masks = lane_masks(keys.shape[1])
    for part, (qkv_ref, o_ref) in enumerate(((qkv_a, oa), (qkv_b, ob))):
        queries = qkv_ref[:, QUERIES]
        mixed = None
        for head, mask in enumerate(masks):
            scores = dot_nt(jnp.where(mask, queries, jnp.zeros_like(queries)), keys) * DH ** (-0.5)
            scores = jnp.where(valid, scores, MASKED)
            top = jnp.max(scores, axis=-1, keepdims=True)
            raised = jnp.exp(scores - top)
            low = (raised * (1.0 / jnp.sum(raised, axis=-1, keepdims=True))).astype(BF16)
            probs[0, head, part] = low
            out = dot_nn(low, values)
            mixed = out if mixed is None else jnp.where(mask, out, mixed)
        o_ref[...] = mixed.astype(BF16)


def attend(counts, slots, near, far, seqs, width):
    half = near.shape[0] // seqs
    heads = width // DH
    pairs = heads // 2
    spec = pl.BlockSpec((half, 3 * PAIR), lambda s, p, c: (s, p))
    out_spec = pl.BlockSpec((half, 2 * DH), lambda s, p, c: (s, p))
    return pl.pallas_call(
        attend_kernel,
        grid_spec=pltpu.PrefetchScalarGridSpec(
            num_scalar_prefetch=1,
            grid=(seqs, pairs),
            in_specs=[pl.BlockSpec((1, 2 * half), lambda s, p, c: (0, 0)), spec, spec],
            out_specs=[
                out_spec,
                out_spec,
                pl.BlockSpec((1, 2, 2, half, 2 * half), lambda s, p, c: (s, p, 0, 0, 0)),
            ],
        ),
        out_shape=[
            jax.ShapeDtypeStruct((seqs * half, width), BF16),
            jax.ShapeDtypeStruct((seqs * half, width), BF16),
            jax.ShapeDtypeStruct((seqs, heads, 2, half, 2 * half), BF16),
        ],
        cost_estimate=pl.CostEstimate(
            flops=16 * seqs * pairs * half * half * 128, bytes_accessed=8 << 20, transcendentals=4 * half * half * heads
        ),
    )(counts, slots, near, far)


def attend_back_kernel(qkv_a, ga, qkv_b, gb, probs, da, db, sums):
    half = qkv_a.shape[0]
    keys = jnp.concatenate([qkv_a[:, KEYS], qkv_b[:, KEYS]], axis=0)
    values = jnp.concatenate([qkv_a[:, VALUES], qkv_b[:, VALUES]], axis=0)
    masks = lane_masks(keys.shape[1])
    grad_k = grad_v = None
    for part, (qkv_ref, g_ref, d_ref) in enumerate(((qkv_a, ga, da), (qkv_b, gb, db))):
        queries = qkv_ref[:, QUERIES]
        grads = g_ref[...]
        dq = dk = dv = None
        for head, mask in enumerate(masks):
            low = probs[0, head, part]
            grad_p = dot_nt(jnp.where(mask, grads, jnp.zeros_like(grads)), values)
            weighted = low.astype(F32) * grad_p
            total = jnp.sum(weighted, axis=-1, keepdims=True)
            grad_s = (weighted - low.astype(F32) * total).astype(BF16)
            dq_h = dot_nn(grad_s, keys)
            dk_h = dot_tn(grad_s, queries)
            dv_h = dot_tn(low, grads)
            dq = dq_h if dq is None else jnp.where(mask, dq_h, dq)
            dk = dk_h if dk is None else jnp.where(mask, dk_h, dk)
            dv = dv_h if dv is None else jnp.where(mask, dv_h, dv)
        d_ref[:, QUERIES] = (dq * DH ** (-0.5)).astype(BF16)
        grad_k = dk if grad_k is None else grad_k + dk
        grad_v = dv if grad_v is None else grad_v + dv
    grad_k = (grad_k * DH ** (-0.5)).astype(BF16)
    grad_v = grad_v.astype(BF16)
    da[:, KEYS] = grad_k[:half]
    db[:, KEYS] = grad_k[half:]
    da[:, VALUES] = grad_v[:half]
    db[:, VALUES] = grad_v[half:]
    both = da[...].astype(F32) + db[...].astype(F32)
    sums[0] = jnp.sum(both, axis=0, keepdims=True)


def attend_back(near, far, grad_near, grad_far, probs, seqs, width):
    half = near.shape[0] // seqs
    heads = width // DH
    pairs = heads // 2
    spec = pl.BlockSpec((half, 3 * PAIR), lambda s, p: (s, p))
    plain = pl.BlockSpec((half, PAIR), lambda s, p: (s, p))
    side = jax.ShapeDtypeStruct((seqs * half, 3 * width), BF16)
    return pl.pallas_call(
        attend_back_kernel,
        grid=(seqs, pairs),
        in_specs=[spec, plain] * 2
        + [pl.BlockSpec((1, 2, 2, half, 2 * half), lambda s, p: (s, p, 0, 0, 0))],
        out_specs=[spec] * 2 + [pl.BlockSpec((1, 1, 3 * PAIR), lambda s, p: (s, 0, p))],
        out_shape=[side] * 2 + [jax.ShapeDtypeStruct((seqs, 1, 3 * width), F32)],
        cost_estimate=pl.CostEstimate(
            flops=40 * seqs * pairs * half * half * 128, bytes_accessed=8 << 20, transcendentals=0
        ),
    )(near, grad_near, far, grad_far, probs)


def by_half(index, own, other, axis):
    return jnp.where(index == 0, jnp.concatenate([own, other], axis), jnp.concatenate([other, own], axis))


def fx_swap(array):
    return lax.ppermute(array, "fx", SWAP)


def after(value, *others):
    return lax.optimization_barrier((value,) + others)[0]


def pack_block(pieces, core):
    mine = jnp.concatenate([own for own, _ in pieces], axis=0)
    theirs = core_swap(jnp.concatenate([other for _, other in pieces], axis=0))
    return by_half(core, mine, theirs, 1)


def tp_turn(array, turn):
    size = lax.axis_size("tp")
    return lax.ppermute(array, "tp", [(at, (at + turn) % size) for at in range(size)]) if turn % size else array


def gather_tp(block):
    return lax.all_gather(block, "tp", axis=0, tiled=True)


def gather_fx(near, fx):
    groups = lax.axis_size("fx")
    if groups == 2:
        return by_half(fx, near, fx_swap(near), 1)
    return lax.all_gather(near, "fx", axis=0, tiled=False).transpose(1, 0, 2).reshape(near.shape[0], -1)


def halves_fx(near):
    rows = near.shape[0] // 2
    return [fx_swap(near[:rows]), fx_swap(near[rows:])] if lax.axis_size("fx") == 2 else []


def join_fx(near, other, fx):
    return by_half(fx, near, jnp.concatenate(other, axis=0), 1) if other else gather_fx(near, fx)


def scatter_fx(product, fx, held):
    groups = lax.axis_size("fx")
    pair = 2 * held
    if groups == 2:
        sends = list(product((1 - fx) * pair, pair).astype(BF16))
        sent = [fx_swap(turn) for turn in sends]

        def own():
            return list(product(fx * pair, pair, sends))

        return sent, own
    whole = product(0, groups * pair).astype(BF16)
    sums = [
        lax.psum_scatter(
            turn.reshape(-1, groups, pair).transpose(1, 0, 2), "fx", scatter_dimension=0, tiled=False
        )
        for turn in whole
    ]
    return sums, lambda: [jnp.zeros(turn.shape, F32) for turn in sums]


def scatter_tp(summed):
    return lax.psum_scatter(summed, "tp", scatter_dimension=0, tiled=True)


def finish_fx(mine, fx, held):
    groups = lax.axis_size("fx")
    pair = 2 * held
    if groups == 2:
        sent = fx_swap(lax.dynamic_slice_in_dim(mine, (1 - fx) * pair, pair, 1))
        keep = lax.dynamic_slice_in_dim(mine, fx * pair, pair, 1)
        return (keep.astype(F32) + sent.astype(F32)).astype(BF16)
    split = mine.reshape(-1, groups, pair).transpose(1, 0, 2)
    return lax.psum_scatter(split, "fx", scatter_dimension=0, tiled=False)


def parts_of(mine, core, ctx, held):
    keep = lax.dynamic_slice_in_dim(mine, core * held, held, 1)
    recv = core_swap(lax.dynamic_slice_in_dim(mine, (1 - core) * held, held, 1))
    both = by_half(core, keep, recv, 0)
    return by_half(ctx, both, ctx_swap(both), 0).reshape(4, -1, held)


def norm_parts(rows):
    mean = jnp.mean(rows, axis=-1, keepdims=True)
    centered = rows - mean
    scale = lax.rsqrt(jnp.mean(centered * centered, axis=-1, keepdims=True) + EPSILON)
    return centered * scale, scale


def norm_back(hat, scale, gain, grads):
    scaled = grads * gain
    grad_rows = scale * (
        scaled
        - jnp.mean(scaled, axis=-1, keepdims=True)
        - hat * jnp.mean(scaled * hat, axis=-1, keepdims=True)
    )
    hat, grads, _ = lax.optimization_barrier((hat, grads, grad_rows))
    return grad_rows, jnp.sum(grads * hat, axis=0), jnp.sum(grads, axis=0)


def gelu_parts(inner):
    cumulative = 0.5 * (1.0 + lax.erf(inner * (0.5**0.5)))
    density = jnp.exp(-0.5 * inner * inner) * 0.3989422804014327
    return (inner * cumulative).astype(BF16), (cumulative + inner * density).astype(BF16)


def on_device(
    layer_in, lengths, cotangent, w_query, w_key, w_value, b_query, b_value, w_out, b_out,
    gain_attn, shift_attn, w_up, b_up, w_down, b_down, gain_ffn, shift_ffn,
):
    core, ctx, tp_at = lax.axis_index("core"), lax.axis_index("ctx"), lax.axis_index("tp")
    fx_at = lax.axis_index("fx")
    fs_at = fx_at * 2 + core
    tp = lax.axis_size("tp")
    fsdp = lax.axis_size("fx") * 2
    fence = lax.optimization_barrier
    seq_count, local_slots, model = layer_in.shape
    held = w_query.shape[0]
    seqs = seq_count // tp
    half = local_slots * tp
    rows = seqs * half
    heads_here = w_query.shape[1] // 4
    units_here = w_up.shape[1] // 4

    def owner(turn):
        return lax.rem(tp_at + turn + tp, tp)

    def by_sequence(array):
        blocks = array.reshape(tp, seqs, local_slots, model)
        turns = [
            tp_turn(lax.dynamic_index_in_dim(blocks, owner(turn), 0, keepdims=False), turn) for turn in range(tp)
        ]
        return jnp.concatenate(turns, axis=1).reshape(rows, model)

    def turns_of(array):
        blocks = array.reshape(seqs, tp, local_slots, model)
        return [tp_turn(blocks[:, turn], -turn) for turn in range(tp)]

    def by_order(turns):
        whole = jnp.zeros((tp,) + turns[0].shape, turns[0].dtype)
        for turn, block in enumerate(turns):
            whole = lax.dynamic_update_index_in_dim(whole, block, owner(turn), 0)
        return whole.reshape(seq_count, local_slots, model)

    def by_turn(array):
        block = lax.broadcasted_iota(jnp.int32, (tp, tp, 1), 0)
        turn = lax.broadcasted_iota(jnp.int32, (tp, tp, 1), 1)
        return jnp.sum(jnp.where(lax.rem(tp_at - turn + tp, tp) == block, array[None], 0.0), axis=1)

    row_at = lax.broadcasted_iota(jnp.int32, (1, half), 1)
    row_slot = lax.rem(tp_at - row_at // local_slots + tp, tp) * local_slots + row_at % local_slots

    def parted(weight, width, axis):
        first = 2 * ctx * width
        parts = [
            lax.dynamic_slice_in_dim(weight, first + side * width, width, axis) for side in (core, 1 - core)
        ]
        return tuple(part.T if axis else part for part in parts)

    flats = (b_query, b_value, b_up, b_out, gain_attn, shift_attn, b_down, gain_ffn, shift_ffn)
    flat_rows = 16
    flat_at = lax.broadcasted_iota(jnp.int32, (flat_rows, held), 0)
    flat_block = jnp.zeros((flat_rows, held), BF16)
    for at, flat in enumerate(flats):
        flat_block = jnp.where(flat_at == at, jnp.pad(flat, (0, held - flat.shape[0]))[None], flat_block)
    first_block = pack_block(
        [parted(w, heads_here, 1) for w in (w_query, w_key, w_value)]
        + [parted(w_out, heads_here, 0), (flat_block, flat_block)],
        core,
    )
    cut = units_here // 2
    up_pair = pack_block([parted(w_up, units_here, 1)], core)
    up_block = gather_fx(up_pair[:cut], fx_at)
    down_block = pack_block([parted(w_down, units_here, 0)], core)
    down_block = jnp.concatenate([down_block, up_pair[cut:]], axis=0)
    own_in = by_sequence(after(layer_in, first_block))
    first_turns = [tp_turn(first_block, turn) for turn in range(tp)]
    up_block, down_block = (after(block, *first_turns) for block in (up_block, down_block))
    up_block, down_block, *first_turns[-1:] = fence([up_block, down_block] + first_turns[-1:])
    first_pack = jnp.stack([gather_fx(turn, fx_at) for turn in first_turns])
    both_near = gather_tp(down_block).reshape(tp, units_here + cut, -1)
    up_first = gather_tp(up_block).reshape(tp, cut, model)
    full_qkv = first_pack[:, : 3 * heads_here].reshape(tp // 2, 2, 3, heads_here, model)
    full_qkv = full_qkv.transpose(0, 2, 1, 3, 4).reshape(-1, model)
    full_out = first_pack[:, 3 * heads_here : 4 * heads_here].reshape(-1, model)
    width = tp * heads_here
    flat_first = 4 * heads_here

    def part_vector(at, size):
        whole = first_pack[:, flat_first + at].reshape(tp, fsdp, held)[:, :, :size].reshape(tp, 4, -1)
        return lax.dynamic_index_in_dim(whole, 2 * ctx + core, 1, keepdims=False).astype(F32)

    def model_vector(at):
        return first_pack[0, flat_first + at].astype(F32)

    sizes = [b_query.shape[0], b_value.shape[0], b_up.shape[0]]
    bias_q, bias_v, bias_up = (part_vector(at, size) for at, size in enumerate(sizes))
    bias_out, gain_one, shift_one, bias_down, gain_two, shift_two = (model_vector(3 + i) for i in range(6))
    bias_up = by_turn(bias_up).reshape(-1)
    bias_qkv = jnp.stack([bias_q, jnp.zeros_like(bias_q), bias_v], axis=1).reshape(tp // 2, 2, 3, heads_here)
    bias_qkv = bias_qkv.transpose(0, 2, 1, 3).reshape(-1)

    own_len = lax.dynamic_slice_in_dim(lengths, tp_at * seqs, seqs)
    all_len = jnp.concatenate([own_len, core_swap(own_len)])
    counts = jnp.stack(
        [
            jnp.clip(all_len - ctx * half, 0, half),
            jnp.clip(all_len - (1 - ctx) * half, 0, half),
        ],
        axis=1,
    )

    near_in, far_in = gather_rows(own_in)
    near_qkv = (dot_nt(near_in, full_qkv) + bias_qkv).astype(BF16)
    far_qkv = (dot_nt(far_in, full_qkv) + bias_qkv).astype(BF16)
    near_attn, far_attn, probs = attend(counts, jnp.tile(row_slot, (1, 2)), near_qkv, far_qkv, 2 * seqs, width)
    near_attn, both_near = fence((near_attn, both_near))
    down_near = both_near[:, :units_here].reshape(tp * units_here, -1)
    up_near = both_near[:, units_here:].reshape(tp * cut, -1)
    projected, _ = reduce_rows(dot_nn(near_attn, full_out), dot_nn(far_attn, full_out))
    projected += bias_out
    hat_one, scale_one = norm_parts(own_in.astype(F32) + projected)
    up_second = [gather_fx(up_near, fx_at)] if fsdp != 4 else [fx_swap(up_near)]
    down_other = halves_fx(down_near)
    hat_one, up_second = fence((hat_one, up_second))
    up_second = by_half(fx_at, up_near, up_second[0], 1) if fsdp == 4 else up_second[0]
    full_up = jnp.concatenate([up_first, up_second.reshape(tp, cut, model)], axis=1).reshape(-1, model)
    normed_one = hat_one * gain_one + shift_one
    near_normed, far_normed, (down_other[:1], _) = gather_rows(normed_one.astype(BF16), (down_other[:1], hat_one))
    near_normed, *down_other[1:] = fence([near_normed] + down_other[1:])
    near_hidden, near_slope = gelu_parts(dot_nt(near_normed, full_up) + bias_up)
    far_hidden, far_slope = gelu_parts(dot_nt(far_normed, full_up) + bias_up)
    full_down = join_fx(down_near, down_other, fx_at)
    ffn, _ = reduce_rows(dot_nn(near_hidden, full_down), dot_nn(far_hidden, full_down))
    ffn += bias_down
    hat_two, scale_two = norm_parts(normed_one + ffn)
    hat_two, own_cot = lax.optimization_barrier((hat_two, by_sequence(cotangent)))
    layer_rows = (hat_two * gain_two + shift_two).astype(BF16)

    row_valid = (ctx * half + row_slot < own_len[:, None]).reshape(rows, 1)
    grad_out = jnp.where(row_valid, own_cot.astype(F32), 0.0)
    grad_two, grad_gain_two, grad_shift_two = norm_back(hat_two, scale_two, gain_two, grad_out)
    grad_ffn = grad_two.astype(BF16)
    grad_b_down = jnp.sum(fence(grad_ffn).astype(F32), axis=0)
    near_gffn, far_gffn, layer_turns = gather_rows(grad_ffn, turns_of(layer_rows))
    near_gpre = (dot_nt(near_gffn, full_down) * near_slope.astype(F32)).astype(BF16)
    far_gpre = (dot_nt(far_gffn, full_down) * far_slope.astype(F32)).astype(BF16)

    def columns(array, start, size):
        return lax.dynamic_slice_in_dim(array, start, size, 1)

    def product(near_left, far_left, near_right, far_right):
        return lambda start, size: (
            dot_tn(near_left, columns(near_right, start, size)) + dot_tn(far_left, columns(far_right, start, size))
        )

    grad_b_up = jnp.sum(near_gpre.astype(F32), axis=0) + jnp.sum(far_gpre.astype(F32), axis=0)

    def product_after(near_left, far_left, near_right, far_right, wait):
        near_left, far_left, _ = fence((near_left, far_left, wait))
        return (dot_tn(far_left, far_right) + dot_tn(near_left, near_right)).astype(BF16)

    normed_sent = far_sums(dot_nn(far_gpre, full_up))
    normed_across = ctx_swap(normed_sent)
    normed_near = near_sums(dot_nn(after(near_gpre, normed_sent), full_up)) + grad_two
    grad_down = product_after(near_hidden, far_hidden, near_gffn, far_gffn, normed_sent)

    groups, pair = fsdp // 2, 2 * held

    def up_product(start, size, wait):
        near_left, far_left, _ = fence((near_gpre, far_gpre, wait))
        return product(near_left, far_left, near_normed, far_normed)(start, size)

    up_sends = []
    if groups == 2:
        up_sends = list(up_product((1 - fx_at) * pair, pair, normed_sent).astype(BF16).reshape(2, -1, pair))
    normed_across, normed_near, grad_down, up_sends = fence((normed_across, normed_near, grad_down, up_sends))
    up_got = [fx_swap(half) for half in up_sends]
    down_mine = scatter_tp(grad_down)
    grad_normed = normed_near + normed_across.astype(F32)
    grad_one, grad_gain_one, grad_shift_one = norm_back(hat_one, scale_one, gain_one, grad_normed)
    grad_proj = grad_one.astype(BF16)
    grad_b_out = jnp.sum(fence(grad_proj).astype(F32), axis=0)
    up_own = up_product(fx_at * pair, pair, grad_proj) if groups == 2 else up_product(0, model, grad_proj)
    near_gproj, far_gproj, (up_own, up_got[:1]) = gather_rows(grad_proj, (up_own, up_got[:1]))
    near_gattn = dot_nt(near_gproj, full_out).astype(BF16)
    far_gattn = dot_nt(far_gproj, full_out).astype(BF16)
    out_product = product(near_attn, far_attn, near_gproj, far_gproj)
    out_early = []
    if groups == 2:
        out_early = [out_product((1 - fx_at) * pair, pair).astype(BF16), out_product(fx_at * pair, pair)]
        near_gattn, far_gattn, out_early = fence((near_gattn, far_gattn, out_early))
    near_dqkv, far_dqkv, bias_sums = attend_back(near_qkv, far_qkv, near_gattn, far_gattn, probs, 2 * seqs, width)
    far_dqkv, up_got = fence((far_dqkv, up_got))
    input_sent = far_sums(dot_nn(far_dqkv, full_qkv))
    if groups == 2:
        up_sum = (up_own + jnp.concatenate(up_got, axis=0).astype(F32)).astype(BF16)
        input_sent, down_mine, up_sum = fence((input_sent, down_mine, up_sum))
        up_mine = scatter_tp(up_sum)
    else:
        up_mine = finish_fx(scatter_tp(up_own.astype(BF16)), fx_at, held)
    bias_sums = after(bias_sums, input_sent)
    grad_b_up = after(grad_b_up, input_sent)
    grad_b_qkv = jnp.sum(bias_sums, axis=0).reshape(tp // 2, 3, 2, heads_here)
    grad_b_q, grad_b_v = grad_b_qkv[:, 0], grad_b_qkv[:, 2]

    model_rows = jnp.stack(
        [grad_b_out, grad_gain_one, grad_shift_one, grad_b_down, grad_gain_two, grad_shift_two]
    )
    part_rows = jnp.concatenate(
        [by_turn(grad_b_up.reshape(tp, -1)), grad_b_q.reshape(tp, -1), grad_b_v.reshape(tp, -1)], axis=1
    )
    spare = -part_rows.shape[1] % held
    part_rows = jnp.pad(part_rows, ((0, 0), (0, spare))).reshape(tp, -1, held)
    part_count = part_rows.shape[1]
    vector_rows = jnp.concatenate(
        [
            jnp.broadcast_to(model_rows[None], (tp, 6, model)),
            jnp.tile(part_rows, (1, 1, fsdp)),
        ],
        axis=1,
    )
    pad = -vector_rows.shape[1] % 16
    vector_rows = jnp.pad(vector_rows, ((0, 0), (0, pad), (0, 0)))

    def attn_product(start, size, wait=None):
        left = after(far_dqkv, *([input_sent] if wait is None else wait))
        grad_qkv = product(near_dqkv, left, near_in, far_in)(start, size)
        grad_qkv = grad_qkv.reshape(tp // 2, 3, 2, heads_here, size).transpose(0, 2, 1, 3, 4)
        early = wait is None and groups == 2
        kind = BF16 if early else F32
        grad_out_w = out_early[0 if early else 1] if groups == 2 else out_product(start, size)
        return jnp.concatenate(
            [
                grad_qkv.reshape(tp, 3 * heads_here, size).astype(kind),
                grad_out_w.reshape(tp, heads_here, size).astype(kind),
                lax.dynamic_slice_in_dim(vector_rows, start, size, 2).astype(kind),
            ],
            axis=1,
        )

    attn_sent, attn_own = scatter_fx(attn_product, fx_at, held)
    input_near = near_sums(dot_nn(after(near_dqkv, input_sent), full_qkv)) + grad_one
    attn_own = attn_own()
    early, late = (2, 1), (3, 0)
    input_across = ctx_swap(input_sent)
    input_across, input_near, attn_own, early_sent, up_mine = fence(
        (input_across, input_near, attn_own, [attn_sent[turn] for turn in early], up_mine)
    )
    down_mine = finish_fx(after(down_mine, input_across), fx_at, held)
    input_turns = turns_of((input_near + input_across.astype(F32)).astype(BF16))

    def to_owner(turn, sent):
        return tp_turn((attn_own[turn] + sent.astype(F32)).astype(BF16), -turn)

    got_first, got_second = (to_owner(turn, sent) for turn, sent in zip(early, early_sent))
    input_turns, got_first, down_mine, late_sent = fence(
        (input_turns, got_first, down_mine, [attn_sent[turn] for turn in late])
    )
    ffn_mine = jnp.concatenate([down_mine, up_mine], axis=0)
    got_late = [to_owner(turn, sent) for turn, sent in zip(late, late_sent)]
    ffn_parts = parts_of(ffn_mine, core, ctx, held)
    got_second, got_late, ffn_parts = fence((got_second, got_late, ffn_parts))
    attn_mine = sum(got.astype(F32) for got in [got_first, got_second] + got_late).astype(BF16)
    input_grad = by_order(input_turns)
    layer_out = by_order([after(block, input_sent) for block in layer_turns])
    ffn_parts, attn_parts = ffn_parts.astype(F32), parts_of(attn_mine, core, ctx, held).astype(F32)
    down_parts, up_parts = ffn_parts[:, :units_here], ffn_parts[:, units_here:]

    def weight_t(block):
        return attn_parts[:, block * heads_here : (block + 1) * heads_here].reshape(-1, held)

    base = 4 * heads_here
    vector_sums = jnp.sum(attn_parts[:, base : base + 6], axis=0)
    part_all = attn_parts[:, base + 6 : base + 6 + part_count].reshape(4, -1)

    part_here = lax.dynamic_index_in_dim(part_all, lax.rem(fs_at, 4), 0, keepdims=False)

    def part_grad(start, size, count):
        if count == size:
            return part_here[start : start + size]
        whole = part_all[:, start : start + size].reshape(-1)
        return lax.dynamic_slice_in_dim(whole, fs_at * count, count)

    grads = (
        weight_t(0).T,
        weight_t(1).T,
        weight_t(2).T,
        part_grad(units_here, heads_here, sizes[0]),
        part_grad(units_here + heads_here, heads_here, sizes[1]),
        weight_t(3),
        vector_sums[0],
        vector_sums[1],
        vector_sums[2],
        up_parts.reshape(-1, held).T,
        part_grad(0, units_here, sizes[2]),
        down_parts.reshape(-1, held),
        vector_sums[3],
        vector_sums[4],
        vector_sums[5],
    )
    return (layer_out, input_grad) + grads


def solution(mesh):
    fsdp, ctx, tp = (mesh.shape[axis] for axis in ("fsdp", "ctx", "tp"))
    split = Mesh(mesh.devices.reshape(fsdp // 2, 2, ctx, tp), ("fx", "core", "ctx", "tp"))
    fs = ("fx", "core")
    rows = P(fs, ("ctx", "tp"), None)
    wide, tall = P(fs, "tp"), P("tp", fs)
    part, model = P(("tp", "fx", "core")), P(fs)
    weights = (wide, wide, wide, part, part, tall, model, model, model, wide, part, tall, model, model, model)
    return jax.shard_map(
        on_device,
        mesh=split,
        in_specs=(rows, P(fs), rows) + weights,
        out_specs=(rows, rows) + weights,
        check_vma=False,
    )
```

```python
import jax
import jax.numpy as jnp
from jax import lax
from jax.experimental import pallas as pl
from jax.experimental.pallas import tpu as pltpu
from jax.sharding import Mesh, PartitionSpec as P

DH = 64
EPSILON = 1e-12
MASKED = -1000000000.0
SWAP = [(0, 1), (1, 0)]
F32 = jnp.float32
BF16 = jnp.bfloat16


def core_swap(array):
    return lax.ppermute(array, "core", SWAP)


def ctx_swap(array):
    return lax.ppermute(array, "ctx", SWAP)


def dot_nt(left, right):
    return lax.dot_general(left, right, (((1,), (1,)), ((), ())), preferred_element_type=F32)


def dot_nn(left, right):
    return lax.dot_general(left, right, (((1,), (0,)), ((), ())), preferred_element_type=F32)


def dot_tn(left, right):
    return lax.dot_general(left, right, (((0,), (0,)), ((), ())), preferred_element_type=F32)


def gather_rows(own, beside=()):
    near = jnp.concatenate([own, core_swap(own)], axis=0)
    across, beside = lax.optimization_barrier((ctx_swap(own), beside))
    far = jnp.concatenate([across, core_swap(across)], axis=0)
    return (near, far, beside) if beside else (near, far)


def far_sums(far):
    rows = far.shape[0] // 2
    return (far[:rows] + core_swap(far[rows:].astype(BF16)).astype(F32)).astype(BF16)


def near_sums(near):
    rows = near.shape[0] // 2
    return near[:rows] + core_swap(near[rows:].astype(BF16)).astype(F32)


def reduce_rows(near, far):
    sent = far_sums(far)
    return near_sums(near) + ctx_swap(sent).astype(F32), sent


def lane_masks(width):
    lane = lax.broadcasted_iota(jnp.int32, (1, width), 1)
    return [(lane // DH) == head for head in range(width // DH)]


PAIR = 2 * DH
QUERIES, KEYS, VALUES = (slice(at * PAIR, (at + 1) * PAIR) for at in range(3))


def attend_kernel(counts, slots, qkv_a, qkv_b, oa, ob, probs):
    half = qkv_a.shape[0]
    seq = pl.program_id(0)
    keys = jnp.concatenate([qkv_a[:, KEYS], qkv_b[:, KEYS]], axis=0)
    values = jnp.concatenate([qkv_a[:, VALUES], qkv_b[:, VALUES]], axis=0)
    row = lax.broadcasted_iota(jnp.int32, (1, 2 * half), 1)
    valid = slots[...] < jnp.where(row < half, counts[seq, 0], counts[seq, 1])
    masks = lane_masks(keys.shape[1])
    for part, (qkv_ref, o_ref) in enumerate(((qkv_a, oa), (qkv_b, ob))):
        queries = qkv_ref[:, QUERIES]
        mixed = None
        for head, mask in enumerate(masks):
            scores = dot_nt(jnp.where(mask, queries, jnp.zeros_like(queries)), keys) * DH ** (-0.5)
            scores = jnp.where(valid, scores, MASKED)
            top = jnp.max(scores, axis=-1, keepdims=True)
            raised = jnp.exp(scores - top)
            low = (raised * (1.0 / jnp.sum(raised, axis=-1, keepdims=True))).astype(BF16)
            probs[0, head, part] = low
            out = dot_nn(low, values)
            mixed = out if mixed is None else jnp.where(mask, out, mixed)
        o_ref[...] = mixed.astype(BF16)


def attend(counts, slots, near, far, seqs, width):
    half = near.shape[0] // seqs
    heads = width // DH
    pairs = heads // 2
    spec = pl.BlockSpec((half, 3 * PAIR), lambda s, p, c: (s, p))
    out_spec = pl.BlockSpec((half, 2 * DH), lambda s, p, c: (s, p))
    return pl.pallas_call(
        attend_kernel,
        grid_spec=pltpu.PrefetchScalarGridSpec(
            num_scalar_prefetch=1,
            grid=(seqs, pairs),
            in_specs=[pl.BlockSpec((1, 2 * half), lambda s, p, c: (0, 0)), spec, spec],
            out_specs=[
                out_spec,
                out_spec,
                pl.BlockSpec((1, 2, 2, half, 2 * half), lambda s, p, c: (s, p, 0, 0, 0)),
            ],
        ),
        out_shape=[
            jax.ShapeDtypeStruct((seqs * half, width), BF16),
            jax.ShapeDtypeStruct((seqs * half, width), BF16),
            jax.ShapeDtypeStruct((seqs, heads, 2, half, 2 * half), BF16),
        ],
        cost_estimate=pl.CostEstimate(
            flops=16 * seqs * pairs * half * half * 128, bytes_accessed=8 << 20, transcendentals=4 * half * half * heads
        ),
    )(counts, slots, near, far)


def attend_back_kernel(qkv_a, ga, qkv_b, gb, probs, da, db, sums):
    half = qkv_a.shape[0]
    keys = jnp.concatenate([qkv_a[:, KEYS], qkv_b[:, KEYS]], axis=0)
    values = jnp.concatenate([qkv_a[:, VALUES], qkv_b[:, VALUES]], axis=0)
    masks = lane_masks(keys.shape[1])
    grad_k = grad_v = None
    for part, (qkv_ref, g_ref, d_ref) in enumerate(((qkv_a, ga, da), (qkv_b, gb, db))):
        queries = qkv_ref[:, QUERIES]
        grads = g_ref[...]
        dq = dk = dv = None
        for head, mask in enumerate(masks):
            low = probs[0, head, part]
            grad_p = dot_nt(jnp.where(mask, grads, jnp.zeros_like(grads)), values)
            weighted = low.astype(F32) * grad_p
            total = jnp.sum(weighted, axis=-1, keepdims=True)
            grad_s = (weighted - low.astype(F32) * total).astype(BF16)
            dq_h = dot_nn(grad_s, keys)
            dk_h = dot_tn(grad_s, queries)
            dv_h = dot_tn(low, grads)
            dq = dq_h if dq is None else jnp.where(mask, dq_h, dq)
            dk = dk_h if dk is None else jnp.where(mask, dk_h, dk)
            dv = dv_h if dv is None else jnp.where(mask, dv_h, dv)
        d_ref[:, QUERIES] = (dq * DH ** (-0.5)).astype(BF16)
        grad_k = dk if grad_k is None else grad_k + dk
        grad_v = dv if grad_v is None else grad_v + dv
    grad_k = (grad_k * DH ** (-0.5)).astype(BF16)
    grad_v = grad_v.astype(BF16)
    da[:, KEYS] = grad_k[:half]
    db[:, KEYS] = grad_k[half:]
    da[:, VALUES] = grad_v[:half]
    db[:, VALUES] = grad_v[half:]
    both = da[...].astype(F32) + db[...].astype(F32)
    sums[0] = jnp.sum(both, axis=0, keepdims=True)


def attend_back(near, far, grad_near, grad_far, probs, seqs, width):
    half = near.shape[0] // seqs
    heads = width // DH
    pairs = heads // 2
    spec = pl.BlockSpec((half, 3 * PAIR), lambda s, p: (s, p))
    plain = pl.BlockSpec((half, PAIR), lambda s, p: (s, p))
    side = jax.ShapeDtypeStruct((seqs * half, 3 * width), BF16)
    return pl.pallas_call(
        attend_back_kernel,
        grid=(seqs, pairs),
        in_specs=[spec, plain] * 2
        + [pl.BlockSpec((1, 2, 2, half, 2 * half), lambda s, p: (s, p, 0, 0, 0))],
        out_specs=[spec] * 2 + [pl.BlockSpec((1, 1, 3 * PAIR), lambda s, p: (s, 0, p))],
        out_shape=[side] * 2 + [jax.ShapeDtypeStruct((seqs, 1, 3 * width), F32)],
        cost_estimate=pl.CostEstimate(
            flops=40 * seqs * pairs * half * half * 128, bytes_accessed=8 << 20, transcendentals=0
        ),
    )(near, grad_near, far, grad_far, probs)


def by_half(index, own, other, axis):
    return jnp.where(index == 0, jnp.concatenate([own, other], axis), jnp.concatenate([other, own], axis))


def fx_swap(array):
    return lax.ppermute(array, "fx", SWAP)


def after(value, *others):
    return lax.optimization_barrier((value,) + others)[0]


def pack_block(pieces, core):
    mine = jnp.concatenate([own for own, _ in pieces], axis=0)
    theirs = core_swap(jnp.concatenate([other for _, other in pieces], axis=0))
    return by_half(core, mine, theirs, 1)


def tp_turn(array, turn):
    size = lax.axis_size("tp")
    return lax.ppermute(array, "tp", [(at, (at + turn) % size) for at in range(size)]) if turn % size else array


def gather_tp(block):
    return lax.all_gather(block, "tp", axis=0, tiled=True)


def gather_fx(near, fx):
    groups = lax.axis_size("fx")
    if groups == 2:
        return by_half(fx, near, fx_swap(near), 1)
    return lax.all_gather(near, "fx", axis=0, tiled=False).transpose(1, 0, 2).reshape(near.shape[0], -1)


def halves_fx(near):
    rows = near.shape[0] // 2
    return [fx_swap(near[:rows]), fx_swap(near[rows:])] if lax.axis_size("fx") == 2 else []


def join_fx(near, other, fx):
    return by_half(fx, near, jnp.concatenate(other, axis=0), 1) if other else gather_fx(near, fx)


def scatter_fx(product, fx, held):
    groups = lax.axis_size("fx")
    pair = 2 * held
    if groups == 2:
        sends = list(product((1 - fx) * pair, pair).astype(BF16))
        sent = [fx_swap(turn) for turn in sends]

        def own():
            return list(product(fx * pair, pair, sends))

        return sent, own
    whole = product(0, groups * pair).astype(BF16)
    sums = [
        lax.psum_scatter(
            turn.reshape(-1, groups, pair).transpose(1, 0, 2), "fx", scatter_dimension=0, tiled=False
        )
        for turn in whole
    ]
    return sums, lambda: [jnp.zeros(turn.shape, F32) for turn in sums]


def scatter_tp(summed):
    return lax.psum_scatter(summed, "tp", scatter_dimension=0, tiled=True)


def finish_fx(mine, fx, held):
    groups = lax.axis_size("fx")
    pair = 2 * held
    if groups == 2:
        sent = fx_swap(lax.dynamic_slice_in_dim(mine, (1 - fx) * pair, pair, 1))
        keep = lax.dynamic_slice_in_dim(mine, fx * pair, pair, 1)
        return (keep.astype(F32) + sent.astype(F32)).astype(BF16)
    split = mine.reshape(-1, groups, pair).transpose(1, 0, 2)
    return lax.psum_scatter(split, "fx", scatter_dimension=0, tiled=False)


def parts_of(mine, core, ctx, held):
    keep = lax.dynamic_slice_in_dim(mine, core * held, held, 1)
    recv = core_swap(lax.dynamic_slice_in_dim(mine, (1 - core) * held, held, 1))
    both = by_half(core, keep, recv, 0)
    return by_half(ctx, both, ctx_swap(both), 0).reshape(4, -1, held)


def norm_parts(rows):
    mean = jnp.mean(rows, axis=-1, keepdims=True)
    centered = rows - mean
    scale = lax.rsqrt(jnp.mean(centered * centered, axis=-1, keepdims=True) + EPSILON)
    return centered * scale, scale


def norm_back(hat, scale, gain, grads):
    scaled = grads * gain
    grad_rows = scale * (
        scaled
        - jnp.mean(scaled, axis=-1, keepdims=True)
        - hat * jnp.mean(scaled * hat, axis=-1, keepdims=True)
    )
    hat, grads, _ = lax.optimization_barrier((hat, grads, grad_rows))
    return grad_rows, jnp.sum(grads * hat, axis=0), jnp.sum(grads, axis=0)


def gelu_parts(inner):
    cumulative = 0.5 * (1.0 + lax.erf(inner * (0.5**0.5)))
    density = jnp.exp(-0.5 * inner * inner) * 0.3989422804014327
    return (inner * cumulative).astype(BF16), (cumulative + inner * density).astype(BF16)


def on_device(
    layer_in, lengths, cotangent, w_query, w_key, w_value, b_query, b_value, w_out, b_out,
    gain_attn, shift_attn, w_up, b_up, w_down, b_down, gain_ffn, shift_ffn,
):
    core, ctx, tp_at = lax.axis_index("core"), lax.axis_index("ctx"), lax.axis_index("tp")
    fx_at = lax.axis_index("fx")
    fs_at = fx_at * 2 + core
    tp = lax.axis_size("tp")
    fsdp = lax.axis_size("fx") * 2
    fence = lax.optimization_barrier
    seq_count, local_slots, model = layer_in.shape
    held = w_query.shape[0]
    seqs = seq_count // tp
    half = local_slots * tp
    rows = seqs * half
    heads_here = w_query.shape[1] // 4
    units_here = w_up.shape[1] // 4

    def owner(turn):
        return lax.rem(tp_at + turn + tp, tp)

    def by_sequence(array):
        blocks = array.reshape(tp, seqs, local_slots, model)
        turns = [
            tp_turn(lax.dynamic_index_in_dim(blocks, owner(turn), 0, keepdims=False), turn) for turn in range(tp)
        ]
        return jnp.concatenate(turns, axis=1).reshape(rows, model)

    def turns_of(array):
        blocks = array.reshape(seqs, tp, local_slots, model)
        return [tp_turn(blocks[:, turn], -turn) for turn in range(tp)]

    def by_order(turns):
        whole = jnp.zeros((tp,) + turns[0].shape, turns[0].dtype)
        for turn, block in enumerate(turns):
            whole = lax.dynamic_update_index_in_dim(whole, block, owner(turn), 0)
        return whole.reshape(seq_count, local_slots, model)

    def by_turn(array):
        block = lax.broadcasted_iota(jnp.int32, (tp, tp, 1), 0)
        turn = lax.broadcasted_iota(jnp.int32, (tp, tp, 1), 1)
        return jnp.sum(jnp.where(lax.rem(tp_at - turn + tp, tp) == block, array[None], 0.0), axis=1)

    row_at = lax.broadcasted_iota(jnp.int32, (1, half), 1)
    row_slot = lax.rem(tp_at - row_at // local_slots + tp, tp) * local_slots + row_at % local_slots

    def parted(weight, width, axis):
        first = 2 * ctx * width
        parts = [
            lax.dynamic_slice_in_dim(weight, first + side * width, width, axis) for side in (core, 1 - core)
        ]
        return tuple(part.T if axis else part for part in parts)

    flats = (b_query, b_value, b_up, b_out, gain_attn, shift_attn, b_down, gain_ffn, shift_ffn)
    flat_rows = 16
    flat_at = lax.broadcasted_iota(jnp.int32, (flat_rows, held), 0)
    flat_block = jnp.zeros((flat_rows, held), BF16)
    for at, flat in enumerate(flats):
        flat_block = jnp.where(flat_at == at, jnp.pad(flat, (0, held - flat.shape[0]))[None], flat_block)
    first_block = pack_block(
        [parted(w, heads_here, 1) for w in (w_query, w_key, w_value)]
        + [parted(w_out, heads_here, 0), (flat_block, flat_block)],
        core,
    )
    cut = units_here // 2
    up_pair = pack_block([parted(w_up, units_here, 1)], core)
    up_block = gather_fx(up_pair[:cut], fx_at)
    down_block = pack_block([parted(w_down, units_here, 0)], core)
    down_block = jnp.concatenate([down_block, up_pair[cut:]], axis=0)
    own_in = by_sequence(after(layer_in, first_block))
    first_turns = [tp_turn(first_block, turn) for turn in range(tp)]
    up_block, down_block = (after(block, *first_turns) for block in (up_block, down_block))
    up_block, down_block, *first_turns[-1:] = fence([up_block, down_block] + first_turns[-1:])
    first_pack = jnp.stack([gather_fx(turn, fx_at) for turn in first_turns])
    both_near = gather_tp(down_block).reshape(tp, units_here + cut, -1)
    up_first = gather_tp(up_block).reshape(tp, cut, model)
    full_qkv = first_pack[:, : 3 * heads_here].reshape(tp // 2, 2, 3, heads_here, model)
    full_qkv = full_qkv.transpose(0, 2, 1, 3, 4).reshape(-1, model)
    full_out = first_pack[:, 3 * heads_here : 4 * heads_here].reshape(-1, model)
    width = tp * heads_here
    flat_first = 4 * heads_here

    def part_vector(at, size):
        whole = first_pack[:, flat_first + at].reshape(tp, fsdp, held)[:, :, :size].reshape(tp, 4, -1)
        return lax.dynamic_index_in_dim(whole, 2 * ctx + core, 1, keepdims=False).astype(F32)

    def model_vector(at):
        return first_pack[0, flat_first + at].astype(F32)

    sizes = [b_query.shape[0], b_value.shape[0], b_up.shape[0]]
    bias_q, bias_v, bias_up = (part_vector(at, size) for at, size in enumerate(sizes))
    bias_out, gain_one, shift_one, bias_down, gain_two, shift_two = (model_vector(3 + i) for i in range(6))
    bias_up = by_turn(bias_up).reshape(-1)
    bias_qkv = jnp.stack([bias_q, jnp.zeros_like(bias_q), bias_v], axis=1).reshape(tp // 2, 2, 3, heads_here)
    bias_qkv = bias_qkv.transpose(0, 2, 1, 3).reshape(-1)

    own_len = lax.dynamic_slice_in_dim(lengths, tp_at * seqs, seqs)
    all_len = jnp.concatenate([own_len, core_swap(own_len)])
    counts = jnp.stack(
        [
            jnp.clip(all_len - ctx * half, 0, half),
            jnp.clip(all_len - (1 - ctx) * half, 0, half),
        ],
        axis=1,
    )

    near_in, far_in = gather_rows(own_in)
    near_qkv = (dot_nt(near_in, full_qkv) + bias_qkv).astype(BF16)
    far_qkv = (dot_nt(far_in, full_qkv) + bias_qkv).astype(BF16)
    near_attn, far_attn, probs = attend(counts, jnp.tile(row_slot, (1, 2)), near_qkv, far_qkv, 2 * seqs, width)
    near_attn, both_near = fence((near_attn, both_near))
    down_near = both_near[:, :units_here].reshape(tp * units_here, -1)
    up_near = both_near[:, units_here:].reshape(tp * cut, -1)
    projected, _ = reduce_rows(dot_nn(near_attn, full_out), dot_nn(far_attn, full_out))
    projected += bias_out
    hat_one, scale_one = norm_parts(own_in.astype(F32) + projected)
    up_second = [gather_fx(up_near, fx_at)] if fsdp != 4 else [fx_swap(up_near)]
    down_other = halves_fx(down_near)
    hat_one, up_second = fence((hat_one, up_second))
    up_second = by_half(fx_at, up_near, up_second[0], 1) if fsdp == 4 else up_second[0]
    full_up = jnp.concatenate([up_first, up_second.reshape(tp, cut, model)], axis=1).reshape(-1, model)
    normed_one = hat_one * gain_one + shift_one
    near_normed, far_normed, (down_other[:1], _) = gather_rows(normed_one.astype(BF16), (down_other[:1], hat_one))
    near_normed, *down_other[1:] = fence([near_normed] + down_other[1:])
    near_hidden, near_slope = gelu_parts(dot_nt(near_normed, full_up) + bias_up)
    far_hidden, far_slope = gelu_parts(dot_nt(far_normed, full_up) + bias_up)
    full_down = join_fx(down_near, down_other, fx_at)
    ffn, _ = reduce_rows(dot_nn(near_hidden, full_down), dot_nn(far_hidden, full_down))
    ffn += bias_down
    hat_two, scale_two = norm_parts(normed_one + ffn)
    hat_two, own_cot = lax.optimization_barrier((hat_two, by_sequence(cotangent)))
    layer_rows = (hat_two * gain_two + shift_two).astype(BF16)

    row_valid = (ctx * half + row_slot < own_len[:, None]).reshape(rows, 1)
    grad_out = jnp.where(row_valid, own_cot.astype(F32), 0.0)
    grad_two, grad_gain_two, grad_shift_two = norm_back(hat_two, scale_two, gain_two, grad_out)
    grad_ffn = grad_two.astype(BF16)
    grad_b_down = jnp.sum(fence(grad_ffn).astype(F32), axis=0)
    near_gffn, far_gffn, layer_turns = gather_rows(grad_ffn, turns_of(layer_rows))
    near_gpre = (dot_nt(near_gffn, full_down) * near_slope.astype(F32)).astype(BF16)
    far_gpre = (dot_nt(far_gffn, full_down) * far_slope.astype(F32)).astype(BF16)

    def columns(array, start, size):
        return lax.dynamic_slice_in_dim(array, start, size, 1)

    def product(near_left, far_left, near_right, far_right):
        return lambda start, size: (
            dot_tn(near_left, columns(near_right, start, size)) + dot_tn(far_left, columns(far_right, start, size))
        )

    grad_b_up = jnp.sum(near_gpre.astype(F32), axis=0) + jnp.sum(far_gpre.astype(F32), axis=0)

    def product_after(near_left, far_left, near_right, far_right, wait):
        near_left, far_left, _ = fence((near_left, far_left, wait))
        return (dot_tn(far_left, far_right) + dot_tn(near_left, near_right)).astype(BF16)

    normed_sent = far_sums(dot_nn(far_gpre, full_up))
    normed_across = ctx_swap(normed_sent)
    normed_near = near_sums(dot_nn(after(near_gpre, normed_sent), full_up)) + grad_two
    grad_down = product_after(near_hidden, far_hidden, near_gffn, far_gffn, normed_sent)

    groups, pair = fsdp // 2, 2 * held

    def up_product(start, size, wait):
        near_left, far_left, _ = fence((near_gpre, far_gpre, wait))
        return product(near_left, far_left, near_normed, far_normed)(start, size)

    up_sends = []
    if groups == 2:
        up_sends = list(up_product((1 - fx_at) * pair, pair, normed_sent).astype(BF16).reshape(2, -1, pair))
    normed_across, normed_near, grad_down, up_sends = fence((normed_across, normed_near, grad_down, up_sends))
    up_got = [fx_swap(half) for half in up_sends]
    down_mine = scatter_tp(grad_down)
    grad_normed = normed_near + normed_across.astype(F32)
    grad_one, grad_gain_one, grad_shift_one = norm_back(hat_one, scale_one, gain_one, grad_normed)
    grad_proj = grad_one.astype(BF16)
    grad_b_out = jnp.sum(fence(grad_proj).astype(F32), axis=0)
    up_own = up_product(fx_at * pair, pair, grad_proj) if groups == 2 else up_product(0, model, grad_proj)
    near_gproj, far_gproj, (up_own, up_got[:1]) = gather_rows(grad_proj, (up_own, up_got[:1]))
    near_gattn = dot_nt(near_gproj, full_out).astype(BF16)
    far_gattn = dot_nt(far_gproj, full_out).astype(BF16)
    out_product = product(near_attn, far_attn, near_gproj, far_gproj)
    out_early = []
    if groups == 2:
        out_early = [out_product((1 - fx_at) * pair, pair).astype(BF16), out_product(fx_at * pair, pair)]
        near_gattn, far_gattn, out_early = fence((near_gattn, far_gattn, out_early))
    near_dqkv, far_dqkv, bias_sums = attend_back(near_qkv, far_qkv, near_gattn, far_gattn, probs, 2 * seqs, width)
    far_dqkv, up_got = fence((far_dqkv, up_got))
    input_sent = far_sums(dot_nn(far_dqkv, full_qkv))
    if groups == 2:
        up_sum = (up_own + jnp.concatenate(up_got, axis=0).astype(F32)).astype(BF16)
        input_sent, down_mine, up_sum = fence((input_sent, down_mine, up_sum))
        up_mine = scatter_tp(up_sum)
    else:
        up_mine = finish_fx(scatter_tp(up_own.astype(BF16)), fx_at, held)
    bias_sums = after(bias_sums, input_sent)
    grad_b_up = after(grad_b_up, input_sent)
    grad_b_qkv = jnp.sum(bias_sums, axis=0).reshape(tp // 2, 3, 2, heads_here)
    grad_b_q, grad_b_v = grad_b_qkv[:, 0], grad_b_qkv[:, 2]

    model_rows = jnp.stack(
        [grad_b_out, grad_gain_one, grad_shift_one, grad_b_down, grad_gain_two, grad_shift_two]
    )
    part_rows = jnp.concatenate(
        [by_turn(grad_b_up.reshape(tp, -1)), grad_b_q.reshape(tp, -1), grad_b_v.reshape(tp, -1)], axis=1
    )
    spare = -part_rows.shape[1] % held
    part_rows = jnp.pad(part_rows, ((0, 0), (0, spare))).reshape(tp, -1, held)
    part_count = part_rows.shape[1]
    vector_rows = jnp.concatenate(
        [
            jnp.broadcast_to(model_rows[None], (tp, 6, model)),
            jnp.tile(part_rows, (1, 1, fsdp)),
        ],
        axis=1,
    )
    pad = -vector_rows.shape[1] % 16
    vector_rows = jnp.pad(vector_rows, ((0, 0), (0, pad), (0, 0)))

    def attn_product(start, size, wait=None):
        left = after(far_dqkv, *([input_sent] if wait is None else wait))
        grad_qkv = product(near_dqkv, left, near_in, far_in)(start, size)
        grad_qkv = grad_qkv.reshape(tp // 2, 3, 2, heads_here, size).transpose(0, 2, 1, 3, 4)
        early = wait is None and groups == 2
        kind = BF16 if early else F32
        grad_out_w = out_early[0 if early else 1] if groups == 2 else out_product(start, size)
        return jnp.concatenate(
            [
                grad_qkv.reshape(tp, 3 * heads_here, size).astype(kind),
                grad_out_w.reshape(tp, heads_here, size).astype(kind),
                lax.dynamic_slice_in_dim(vector_rows, start, size, 2).astype(kind),
            ],
            axis=1,
        )

    attn_sent, attn_own = scatter_fx(attn_product, fx_at, held)
    input_near = near_sums(dot_nn(after(near_dqkv, input_sent), full_qkv)) + grad_one
    attn_own = attn_own()
    early, late = (1, 3), (2, 0)
    input_across = ctx_swap(input_sent)
    input_across, input_near, attn_own, early_sent, up_mine = fence(
        (input_across, input_near, attn_own, [attn_sent[turn] for turn in early], up_mine)
    )
    down_mine = finish_fx(after(down_mine, input_across), fx_at, held)
    input_turns = turns_of((input_near + input_across.astype(F32)).astype(BF16))

    def to_owner(turn, sent):
        return tp_turn((attn_own[turn] + sent.astype(F32)).astype(BF16), -turn)

    got_first, got_second = (to_owner(turn, sent) for turn, sent in zip(early, early_sent))
    input_turns, got_first, down_mine, late_sent = fence(
        (input_turns, got_first, down_mine, [attn_sent[turn] for turn in late])
    )
    ffn_mine = jnp.concatenate([down_mine, up_mine], axis=0)
    got_late = [to_owner(turn, sent) for turn, sent in zip(late, late_sent)]
    ffn_parts = parts_of(ffn_mine, core, ctx, held)
    got_second, got_late, ffn_parts = fence((got_second, got_late, ffn_parts))
    attn_mine = sum(got.astype(F32) for got in [got_first, got_second] + got_late).astype(BF16)
    input_grad = by_order(input_turns)
    layer_out = by_order([after(block, input_sent) for block in layer_turns])
    ffn_parts, attn_parts = ffn_parts.astype(F32), parts_of(attn_mine, core, ctx, held).astype(F32)
    down_parts, up_parts = ffn_parts[:, :units_here], ffn_parts[:, units_here:]

    def weight_t(block):
        return attn_parts[:, block * heads_here : (block + 1) * heads_here].reshape(-1, held)

    base = 4 * heads_here
    vector_sums = jnp.sum(attn_parts[:, base : base + 6], axis=0)
    part_all = attn_parts[:, base + 6 : base + 6 + part_count].reshape(4, -1)

    part_here = lax.dynamic_index_in_dim(part_all, lax.rem(fs_at, 4), 0, keepdims=False)

    def part_grad(start, size, count):
        if count == size:
            return part_here[start : start + size]
        whole = part_all[:, start : start + size].reshape(-1)
        return lax.dynamic_slice_in_dim(whole, fs_at * count, count)

    grads = (
        weight_t(0).T,
        weight_t(1).T,
        weight_t(2).T,
        part_grad(units_here, heads_here, sizes[0]),
        part_grad(units_here + heads_here, heads_here, sizes[1]),
        weight_t(3),
        vector_sums[0],
        vector_sums[1],
        vector_sums[2],
        up_parts.reshape(-1, held).T,
        part_grad(0, units_here, sizes[2]),
        down_parts.reshape(-1, held),
        vector_sums[3],
        vector_sums[4],
        vector_sums[5],
    )
    return (layer_out, input_grad) + grads


def solution(mesh):
    fsdp, ctx, tp = (mesh.shape[axis] for axis in ("fsdp", "ctx", "tp"))
    split = Mesh(mesh.devices.reshape(fsdp // 2, 2, ctx, tp), ("fx", "core", "ctx", "tp"))
    fs = ("fx", "core")
    rows = P(fs, ("ctx", "tp"), None)
    wide, tall = P(fs, "tp"), P("tp", fs)
    part, model = P(("tp", "fx", "core")), P(fs)
    weights = (wide, wide, wide, part, part, tall, model, model, model, wide, part, tall, model, model, model)
    return jax.shard_map(
        on_device,
        mesh=split,
        in_specs=(rows, P(fs), rows) + weights,
        out_specs=(rows, rows) + weights,
        check_vma=False,
    )
```
